32 devices in a mesh: group: 8 (over z, x), dom: 4 (over y, core).
Axes of the slice: x: 2, y: 2, z: 4, core: 2. Of those that a mesh axis runs over, the one named last changes fastest.
Arguments:
- features: bfloat16 [65536, 128], P(('group', 'dom')), may hold values from -6 to 6
- w_in: bfloat16 [128, 1024], replicated, may hold values from -0.5 to 0.5
- b_in: float32 [1024], replicated, may hold values from -4 to 4
- w_out: bfloat16 [1024, 128], replicated, may hold values from -0.1875 to 0.1875
- anchor_ids: int32 [131072], P(('group', 'dom')), may hold values from 0 to 8191
- local_tiles: int32 [1024, 4], P(('group', 'dom')), may hold values from 0 to 63
- requests: int32 [8, 4, 8, 8], P('group', 'dom'), may hold values from 0 to 63
- counts: int32 [8, 4, 8], P('group', 'dom'), may hold values from 0 to 8, as said below
- remote_refs: int32 [1024, 4], P(('group', 'dom')), may hold values from 0 to 63
- teacher: bfloat16 [131072, 1024], P(('group', 'dom')), may hold values from -12 to 12
Outputs:
- anchor_kl: float32 [131072], P(('group', 'dom'))
- node_grad: float32 [65536, 128], P(('group', 'dom'))
- grad_w_in: float32 [128, 1024], replicated
- grad_b_in: float32 [1024], replicated
- grad_w_out: float32 [1024, 128], replicated
The draws below stay inside these ranges and needn't reach their ends.
Inputs may be any that keep to these rules, and one draw needn't show every extreme that they name: `requests`: slots at or past the count hold tile numbers too. counts[g, d, g] is 0; in every draw some device has 8 live slots from every other group.
All inputs are finite; a program needn't handle non-finite values.
Results may differ from the reference program's by a relative error of at most 0.0067.
Values may be sent and summed in bfloat16 or wider, within the bound.
A program may use at most 192 MiB of HBM per device.

```python
import jax
import jax.numpy as jnp
from jax import lax

F = 128
HID = 1024
EMB = 128
TILE = 128
NODE_DEV = 2048
ANCH_DEV = 4096
ABLK = 128
LOC_T = 4
REM_T = 4
CAP = 8
GROUP_NODES = 8192
GROUP_TILES = 64
NODES = 65536
ANCHORS = 131072
BLOCKS = 1024
CTX = 1024
N_GROUP = 8
N_DOM = 4


def draw_counts(key, part):
    base_key = jax.random.fold_in(key, 11)
    key_list = jax.random.split(base_key, 4)
    base_counts = jax.random.randint(key_list[0], (N_GROUP, N_DOM, N_GROUP), 1, CAP // 2 + 1)
    hot_rows = jax.random.randint(key_list[1], (N_GROUP, N_DOM, 1), 0, 8) == 0
    forced_group = jax.random.randint(key_list[2], (), 0, N_GROUP)
    forced_dom = jax.random.randint(key_list[3], (), 0, N_DOM)
    group_iota = jnp.arange(N_GROUP)[:, None, None]
    dom_iota = jnp.arange(N_DOM)[None, :, None]
    source_iota = jnp.arange(N_GROUP)[None, None, :]
    forced = (group_iota == forced_group) & (dom_iota == forced_dom)
    full_rows = hot_rows | forced
    counts_all = jnp.where(full_rows, CAP, base_counts)
    return jnp.where(group_iota == source_iota, 0, counts_all).astype(jnp.int32)


def set_ends(entries, rng, low, largest):
    extent = entries.shape
    place = [jax.random.randint(jax.random.fold_in(rng, axis), (), 0, extent[axis]) for axis in range(len(extent))]
    entries = entries.at[tuple(place)].set(low)
    longest = extent.index(max(extent))
    place[longest] = (place[longest] + 1) % extent[longest]
    return entries.at[tuple(place)].set(largest)


def block_scale(key, extent, cuts, least, high):
    factor_of = 1.0
    for axis_at, blocks in cuts:
        steps = jax.random.uniform(jax.random.fold_in(jax.random.fold_in(key, 6), axis_at), (blocks,), jnp.float32, least / len(cuts), high / len(cuts))
        factor_of = factor_of * jnp.repeat(jnp.exp(steps), extent[axis_at] // blocks).reshape((-1,) + (1,) * (len(extent) - 1 - axis_at))
    return factor_of


def scatter_about(key, extent, scale, limit, cuts=(), kind=jnp.bfloat16):
    entries = jax.random.normal(key, extent, jnp.float32) * scale
    if len(cuts) > 0:
        entries = block_scale(key, extent, cuts, -0.22, 0.18) * entries
    return jnp.clip(entries, min=-limit, max=limit).astype(kind)


def setup_inputs(seed: int = 0) -> dict:
    streams_of = jax.random.split(jax.random.key(seed), 11)
    return {
        "features": scatter_about(streams_of[0], (NODES, F), 1.0, 6.0, ((0, 32),)),
        "w_in": scatter_about(streams_of[1], (F, HID), F ** -0.5, 0.5),
        "b_in": scatter_about(streams_of[2], (HID,), 1.0, 4.0, (), jnp.float32),
        "w_out": scatter_about(streams_of[3], (HID, EMB), HID ** -0.5, 0.1875),
        "anchor_ids": set_ends(jax.random.randint(streams_of[4], (ANCHORS,), 0, GROUP_NODES), jax.random.fold_in(streams_of[4], 1), 0, GROUP_NODES - 1).astype(jnp.int32),
        "local_tiles": set_ends(jax.random.randint(streams_of[5], (BLOCKS, LOC_T), 0, GROUP_TILES), jax.random.fold_in(streams_of[5], 1), 0, GROUP_TILES - 1).astype(jnp.int32),
        "requests": set_ends(jax.random.randint(streams_of[6], (N_GROUP, N_DOM, N_GROUP, CAP), 0, GROUP_TILES), jax.random.fold_in(streams_of[6], 1), 0, GROUP_TILES - 1).astype(jnp.int32),
        "counts": draw_counts(jax.random.fold_in(streams_of[10], 71), 0),
        "remote_refs": set_ends(jax.random.randint(streams_of[8], (BLOCKS, REM_T), 0, N_GROUP * CAP), jax.random.fold_in(streams_of[8], 1), 0, (N_GROUP * CAP) - 1).astype(jnp.int32),
        "teacher": scatter_about(streams_of[9], (ANCHORS, CTX), 3.0, 12.0, ((0, 32),)),
    }


SCORE_SCALE = 8.0
EPSILON = 1e-06

def node_forward(feature_rows, w_in, b_in, w_out):
    pre_act = jnp.dot(feature_rows, w_in, preferred_element_type=jnp.float32) + b_in
    hidden = jax.nn.silu(pre_act).astype(jnp.bfloat16)
    embedding = jnp.dot(hidden, w_out, preferred_element_type=jnp.float32)
    spread = jnp.sqrt(lax.optimization_barrier(jnp.mean(embedding * embedding, axis=1, keepdims=True)) + EPSILON)
    unit_rows = (embedding / spread).astype(jnp.bfloat16)
    return (pre_act, hidden, embedding, spread, unit_rows)

def reference(features, w_in, b_in, w_out, anchor_ids, local_tiles, requests, counts, remote_refs, teacher):
    devices = N_GROUP * N_DOM
    per_device = ANCH_DEV // ABLK
    feature_blocks = features.reshape(devices, NODE_DEV, F)
    unit_all = lax.map(lambda rows_in: node_forward(rows_in, w_in, b_in, w_out)[4], feature_blocks).reshape(NODES, EMB)
    tile_iota = jnp.arange(TILE, dtype=jnp.int32)
    score_scale = SCORE_SCALE / EMB

    def score_device(grad_rows, inputs):
        device_index, anchor_block, local_block, remote_block, teacher_block = inputs
        group_index = device_index // N_DOM
        dom_index = device_index % N_DOM
        group_base = group_index * GROUP_NODES
        own_requests = requests[group_index, dom_index]
        own_counts = counts[group_index, dom_index]
        source_group = remote_block // CAP
        slot_index = remote_block % CAP
        tile_numbers = own_requests[source_group, slot_index]
        remote_live = slot_index < own_counts[source_group]
        local_rows = group_base + local_block[:, :, None] * TILE + tile_iota
        remote_rows = source_group[:, :, None] * GROUP_NODES + tile_numbers[:, :, None] * TILE + tile_iota
        context_rows = jnp.concatenate([local_rows, remote_rows], axis=1).reshape(per_device, CTX)
        live_tiles = jnp.concatenate([jnp.ones((per_device, LOC_T), jnp.bool_), remote_live], axis=1)
        live_mask = jnp.repeat(live_tiles, TILE, axis=1).astype(jnp.float32)[:, None, :]
        anchor_rows = group_base + anchor_block
        anchor_vecs = unit_all[anchor_rows].astype(jnp.float32)
        context_vecs = unit_all[context_rows].astype(jnp.float32)
        scores = jnp.einsum('bae,bce->bac', anchor_vecs, context_vecs) * score_scale
        student_exp = jnp.exp(scores) * live_mask
        student_total = lax.optimization_barrier(jnp.sum(student_exp, axis=2, keepdims=True))
        teacher_f = teacher_block.astype(jnp.float32)
        target_exp = jnp.exp(teacher_f) * live_mask
        target_total = lax.optimization_barrier(jnp.sum(target_exp, axis=2, keepdims=True))
        target_prob = target_exp / target_total
        divergence = lax.optimization_barrier(jnp.sum(target_prob * (teacher_f - scores), axis=2)) - jnp.log(target_total[:, :, 0]) + jnp.log(student_total[:, :, 0])
        prob_delta = (student_exp / student_total - target_prob).astype(jnp.bfloat16).astype(jnp.float32)
        anchor_grad = jnp.einsum('bac,bce->bae', prob_delta, context_vecs) * score_scale
        context_grad = jnp.einsum('bac,bae->bce', prob_delta, anchor_vecs) * score_scale
        grad_rows = grad_rows.at[anchor_rows.reshape(-1)].add(anchor_grad.reshape(-1, EMB))
        grad_rows = grad_rows.at[context_rows.reshape(-1)].add(context_grad.reshape(-1, EMB))
        return (grad_rows, divergence)
    score_inputs = (jnp.arange(devices, dtype=jnp.int32), anchor_ids.reshape(devices, per_device, ABLK), local_tiles.reshape(devices, per_device, LOC_T), remote_refs.reshape(devices, per_device, REM_T), teacher.reshape(devices, per_device, ABLK, CTX))
    node_grad, divergence = lax.scan(score_device, jnp.zeros((NODES, EMB), jnp.float32), score_inputs)
    anchor_kl = divergence.reshape(ANCHORS)

    def backward_device(totals, inputs):
        feature_rows, unit_grad = inputs
        pre_act, hidden, embedding, spread, unit_rows = node_forward(feature_rows, w_in, b_in, w_out)
        normed = embedding / spread
        embed_grad = ((unit_grad - normed * lax.optimization_barrier(jnp.mean(unit_grad * normed, axis=1, keepdims=True))) / spread).astype(jnp.bfloat16)
        out_grad = jnp.dot(hidden.T, embed_grad, preferred_element_type=jnp.float32)
        hidden_grad = jnp.dot(embed_grad, w_out.T, preferred_element_type=jnp.float32)
        sigmoid_pre = jax.nn.sigmoid(pre_act)
        pre_grad = hidden_grad * sigmoid_pre * (1.0 + pre_act * (1.0 - sigmoid_pre))
        bias_grad = lax.optimization_barrier(jnp.sum(pre_grad, axis=0))
        in_grad = jnp.dot(feature_rows.T, pre_grad.astype(jnp.bfloat16), preferred_element_type=jnp.float32)
        return ((totals[0] + in_grad, totals[1] + bias_grad, totals[2] + out_grad), None)
    start_totals = (jnp.zeros((F, HID), jnp.float32), jnp.zeros((HID,), jnp.float32), jnp.zeros((HID, EMB), jnp.float32))
    totals, unused = lax.scan(backward_device, start_totals, (feature_blocks, node_grad.reshape(devices, NODE_DEV, EMB)))
    inverse = 1.0 / devices
    return (anchor_kl, node_grad, totals[0] * inverse, totals[1] * inverse, totals[2] * inverse)
```

```python
import functools

import jax
import jax.numpy as jnp
from jax import lax
from jax.experimental import pallas as pl
from jax.experimental.pallas import tpu as pltpu
from jax.sharding import PartitionSpec as P

TILE = 128
ABLK = 128

SCORE_SCALE = 8.0
EPSILON = 1e-06
VMEM_LIMIT = 60 * 1024 * 1024
CHUNK = 256

ONE_COPY = pl.Buffered(1)


def whole(shape):
    return pl.BlockSpec(shape, lambda *_: (0,) * len(shape), pipeline_mode=ONE_COPY)


def node_forward(feature_rows, w_in, b_in, w_out):
    pre_act = jnp.dot(feature_rows, w_in, preferred_element_type=jnp.float32) + b_in
    hidden = jax.nn.silu(pre_act).astype(jnp.bfloat16)
    embedding = jnp.dot(hidden, w_out, preferred_element_type=jnp.float32)
    spread = jnp.sqrt(jnp.mean(embedding * embedding, axis=1, keepdims=True) + EPSILON)
    unit_rows = (embedding / spread).astype(jnp.bfloat16)
    return (pre_act, hidden, embedding, spread, unit_rows)


def rows_of(index, count=TILE):
    return pl.ds(pl.multiple_of(index * count, count), count)


def pick_kernel(asked_ref, table_ref, out_ref):
    def step(slot, carry):
        out_ref[rows_of(slot), :] = table_ref[rows_of(asked_ref[slot]), :]
        return carry

    lax.fori_loop(0, out_ref.shape[0] // TILE, step, 0, unroll=2)


def pick_tiles(asked, table, slots):
    shape = (slots * TILE, table.shape[1])
    return pl.pallas_call(
        pick_kernel,
        out_shape=jax.ShapeDtypeStruct(shape, table.dtype),
        grid_spec=pltpu.PrefetchScalarGridSpec(
            num_scalar_prefetch=1,
            grid=(1,),
            in_specs=[whole(table.shape)],
            out_specs=whole(shape),
        ),
        compiler_params=pltpu.CompilerParams(vmem_limit_bytes=VMEM_LIMIT),
    )(asked, table)


def score_kernel(
    local_count,
    remote_count,
    slot_count,
    lanes,
    ids_ref,
    tiles_ref,
    refs_ref,
    counts_ref,
    table_ref,
    fetched_ref,
    teacher_ref,
    kl_ref,
    local_grad_ref,
    remote_grad_ref,
    table_f,
    remote_acc,
    context,
    delta,
    anchor_rows,
    anchor_grad,
    *row_accs,
):
    block = pl.program_id(0)
    width = table_ref.shape[1]
    scale = SCORE_SCALE / width
    zero_chunk = jnp.zeros((CHUNK, width), jnp.float32)

    @pl.when(block == 0)
    def _():
        def clear(index, carry):
            here = rows_of(index, CHUNK)
            table_f[here, :] = table_ref[here, :].astype(jnp.float32)
            local_grad_ref[here, :] = zero_chunk
            for acc in row_accs:
                acc[here, :] = zero_chunk
            return carry

        lax.fori_loop(0, table_f.shape[0] // CHUNK, clear, 0)

        def clear_remote(index, carry):
            remote_acc[rows_of(index, CHUNK), :] = zero_chunk
            return carry

        lax.fori_loop(0, remote_acc.shape[0] // CHUNK, clear_remote, 0)

    rows = [ids_ref[block * ABLK + row] for row in range(ABLK)]
    for row in range(ABLK):
        anchor_rows[row : row + 1, :] = table_f[pl.ds(rows[row], 1), :]
    anchors = (anchor_rows[...] * scale).astype(jnp.bfloat16)

    places = []
    lives = []
    for i in range(local_count):
        place = rows_of(tiles_ref[block * local_count + i])
        context[i * TILE : (i + 1) * TILE, :] = table_ref[place, :]
        places.append(place)
        lives.append(None)
    for i in range(remote_count):
        ref = refs_ref[block * remote_count + i]
        place = rows_of(ref)
        at = local_count + i
        context[at * TILE : (at + 1) * TILE, :] = fetched_ref[place, :]
        places.append(place)
        live = lax.rem(ref, slot_count) < counts_ref[lax.div(ref, slot_count)]
        lives.append(jnp.where(live, 1.0, 0.0).astype(jnp.float32))

    student = []
    target = []
    student_sum = target_sum = gap_sum = None
    for i in range(local_count + remote_count):
        span = slice(i * TILE, (i + 1) * TILE)
        scores = lax.dot_general(
            anchors,
            context[span, :],
            (((1,), (1,)), ((), ())),
            preferred_element_type=jnp.float32,
        )
        teacher = teacher_ref[:, span].astype(jnp.float32)
        student_exp = jnp.exp(scores)
        target_exp = jnp.exp(teacher)
        if lives[i] is not None:
            student_exp = student_exp * lives[i]
            target_exp = target_exp * lives[i]
        gap = target_exp * (teacher - scores)
        student_sum = student_exp if i == 0 else student_sum + student_exp
        target_sum = target_exp if i == 0 else target_sum + target_exp
        gap_sum = gap if i == 0 else gap_sum + gap
        student.append(student_exp)
        target.append(target_exp)
    student_total = jnp.sum(student_sum, axis=1, keepdims=True)
    target_total = jnp.sum(target_sum, axis=1, keepdims=True)
    gap_total = jnp.sum(gap_sum, axis=1, keepdims=True)
    student_inv = 1.0 / student_total
    target_inv = 1.0 / target_total
    divergence = gap_total * target_inv - jnp.log(target_total) + jnp.log(student_total)
    kl_ref[0] = jnp.broadcast_to(divergence, (ABLK, TILE)).T[0:1, :]
    for i in range(local_count + remote_count):
        span = slice(i * TILE, (i + 1) * TILE)
        delta[:, span] = (student[i] * student_inv - target[i] * target_inv).astype(jnp.bfloat16)
    anchor_grad[...] = (
        jnp.dot(delta[...], context[...], preferred_element_type=jnp.float32) * scale
    )
    for i in range(local_count + remote_count):
        span = slice(i * TILE, (i + 1) * TILE)
        context_grad = lax.dot_general(
            delta[:, span],
            anchors,
            (((0,), (0,)), ((), ())),
            preferred_element_type=jnp.float32,
        )
        acc = local_grad_ref if i < local_count else remote_acc
        acc[places[i], :] += context_grad
    for row in range(ABLK):
        acc = row_accs[row % lanes]
        acc[pl.ds(rows[row], 1), :] += anchor_grad[row : row + 1, :]

    @pl.when(block == pl.num_programs(0) - 1)
    def _():
        def finish(index, carry):
            here = rows_of(index, CHUNK)
            total = local_grad_ref[here, :]
            for acc in row_accs:
                total = total + acc[here, :]
            local_grad_ref[here, :] = total
            return carry

        lax.fori_loop(0, table_f.shape[0] // CHUNK, finish, 0)

        def finish_remote(index, carry):
            here = rows_of(index, CHUNK)
            remote_grad_ref[here, :] = remote_acc[here, :].astype(jnp.bfloat16)
            return carry

        lax.fori_loop(0, remote_acc.shape[0] // CHUNK, finish_remote, 0)


def score(anchor_ids, local_tiles, remote_refs, own_counts, table, fetched, teacher, slot_count):
    blocks, local_count = local_tiles.shape
    remote_count = remote_refs.shape[1]
    context_width = teacher.shape[1]
    width = table.shape[1]
    lanes = 4 if table.shape[0] <= 8192 else 1
    kernel = functools.partial(score_kernel, local_count, remote_count, slot_count, lanes)
    kl, local_grad, remote_grad = pl.pallas_call(
        kernel,
        out_shape=(
            jax.ShapeDtypeStruct((blocks, 1, ABLK), jnp.float32),
            jax.ShapeDtypeStruct(table.shape, jnp.float32),
            jax.ShapeDtypeStruct(fetched.shape, jnp.bfloat16),
        ),
        grid_spec=pltpu.PrefetchScalarGridSpec(
            num_scalar_prefetch=4,
            grid=(blocks,),
            in_specs=[
                whole(table.shape),
                whole(fetched.shape),
                pl.BlockSpec((ABLK, context_width), lambda b, *_: (b, 0)),
            ],
            out_specs=(
                pl.BlockSpec((1, 1, ABLK), lambda b, *_: (b, 0, 0)),
                whole(table.shape),
                whole(fetched.shape),
            ),
            scratch_shapes=[
                pltpu.VMEM(table.shape, jnp.float32),
                pltpu.VMEM(fetched.shape, jnp.float32),
                pltpu.VMEM((context_width, width), jnp.bfloat16),
                pltpu.VMEM((ABLK, context_width), jnp.bfloat16),
                pltpu.VMEM((ABLK, width), jnp.float32),
                pltpu.VMEM((ABLK, width), jnp.float32),
            ]
            + [pltpu.VMEM(table.shape, jnp.float32)] * lanes,
        ),
        compiler_params=pltpu.CompilerParams(vmem_limit_bytes=VMEM_LIMIT),
    )(
        anchor_ids,
        local_tiles.reshape(-1),
        remote_refs.reshape(-1),
        own_counts,
        table,
        fetched,
        teacher,
    )
    return kl.reshape(-1), local_grad, remote_grad


def merge_kernel(asked_ref, local_ref, returned_ref, out_ref, acc):
    def load(index, carry):
        here = rows_of(index, CHUNK)
        acc[here, :] = local_ref[here, :]
        return carry

    lax.fori_loop(0, acc.shape[0] // CHUNK, load, 0)

    def add(slot, carry):
        acc[rows_of(asked_ref[slot]), :] += returned_ref[rows_of(slot), :].astype(jnp.float32)
        return carry

    lax.fori_loop(0, returned_ref.shape[0] // TILE, add, 0)

    def store(index, carry):
        here = rows_of(index, CHUNK)
        out_ref[here, :] = acc[here, :].astype(jnp.bfloat16)
        return carry

    lax.fori_loop(0, acc.shape[0] // CHUNK, store, 0)


def merge(asked, local_grad, returned):
    return pl.pallas_call(
        merge_kernel,
        out_shape=jax.ShapeDtypeStruct(local_grad.shape, jnp.bfloat16),
        grid_spec=pltpu.PrefetchScalarGridSpec(
            num_scalar_prefetch=1,
            grid=(1,),
            in_specs=[whole(local_grad.shape), whole(returned.shape)],
            out_specs=whole(local_grad.shape),
            scratch_shapes=[pltpu.VMEM(local_grad.shape, jnp.float32)],
        ),
        compiler_params=pltpu.CompilerParams(vmem_limit_bytes=VMEM_LIMIT),
    )(asked, local_grad, returned)


def shards(
    features, w_in, b_in, w_out, anchor_ids, local_tiles, requests, counts, remote_refs, teacher
):
    groups = lax.axis_size("group")
    devices = groups * lax.axis_size("dom")
    own_requests = requests[0, 0]
    own_counts = counts[0, 0]
    slot_count = own_requests.shape[1]
    every_request = lax.all_gather(own_requests, "group", axis=0, tiled=False)
    asked = lax.dynamic_index_in_dim(
        every_request, lax.axis_index("group"), axis=1, keepdims=False
    ).reshape(-1)
    pre_act, hidden, embedding, spread, unit_rows = node_forward(features, w_in, b_in, w_out)
    table = lax.all_gather(unit_rows, "dom", axis=0, tiled=True)
    served = pick_tiles(asked, table, groups * slot_count)
    fetched = lax.all_to_all(served, "group", split_axis=0, concat_axis=0, tiled=True)
    anchor_kl, local_grad, remote_grad = score(
        anchor_ids, local_tiles, remote_refs, own_counts, table, fetched, teacher, slot_count
    )
    returned = lax.all_to_all(remote_grad, "group", split_axis=0, concat_axis=0, tiled=True)
    merged = merge(asked, local_grad, returned)
    node_grad = lax.psum_scatter(merged, "dom", scatter_dimension=0, tiled=True).astype(
        jnp.float32
    )
    normed = embedding / spread
    embed_grad = (
        (node_grad - normed * jnp.mean(node_grad * normed, axis=1, keepdims=True)) / spread
    ).astype(jnp.bfloat16)
    out_grad = jnp.dot(hidden.T, embed_grad, preferred_element_type=jnp.float32)
    hidden_grad = jnp.dot(embed_grad, w_out.T, preferred_element_type=jnp.float32)
    sigmoid_pre = jax.nn.sigmoid(pre_act)
    pre_grad = hidden_grad * sigmoid_pre * (1.0 + pre_act * (1.0 - sigmoid_pre))
    bias_grad = jnp.sum(pre_grad, axis=0)
    in_grad_t = jnp.dot(
        pre_grad.astype(jnp.bfloat16).T, features, preferred_element_type=jnp.float32
    )
    hid = in_grad_t.shape[0]
    width = out_grad.shape[1]
    bias_rows = bias_grad.reshape(-1, width)
    used = 2 * hid + bias_rows.shape[0]
    unit = devices * 16
    padding = -used % unit
    stacked = jnp.concatenate(
        [in_grad_t, out_grad, bias_rows, jnp.zeros((padding, width), jnp.float32)], axis=0
    )
    part = lax.psum_scatter(stacked, "dom", scatter_dimension=0, tiled=True)
    part = lax.psum_scatter(part, "group", scatter_dimension=0, tiled=True)
    part = part * (1.0 / devices)
    part = lax.all_gather(part, "group", axis=0, tiled=True)
    totals = lax.all_gather(part, "dom", axis=0, tiled=True)
    return (
        anchor_kl,
        node_grad,
        totals[:hid].T,
        totals[2 * hid : used].reshape(-1),
        totals[hid : 2 * hid],
    )


def solution(mesh):
    return jax.shard_map(
        shards,
        mesh=mesh,
        in_specs=(
            P(("group", "dom"), None),
            P(),
            P(),
            P(),
            P(("group", "dom")),
            P(("group", "dom"), None),
            P("group", "dom", None, None),
            P("group", "dom", None),
            P(("group", "dom"), None),
            P(("group", "dom"), None),
        ),
        out_specs=(P(("group", "dom")), P(("group", "dom"), None), P(), P(), P()),
        check_vma=False,
    )
```

```python
import functools

import jax
import jax.numpy as jnp
from jax import lax
from jax.experimental import pallas as pl
from jax.experimental.pallas import tpu as pltpu
from jax.sharding import PartitionSpec as P

TILE = 128
ABLK = 128

SCORE_SCALE = 8.0
EPSILON = 1e-06
VMEM_LIMIT = 60 * 1024 * 1024
CHUNK = 256

ONE_COPY = pl.Buffered(1)


def whole(shape):
    return pl.BlockSpec(shape, lambda *_: (0,) * len(shape), pipeline_mode=ONE_COPY)


def node_forward(feature_rows, w_in, b_in, w_out):
    pre_act = jnp.dot(feature_rows, w_in, preferred_element_type=jnp.float32) + b_in
    hidden = jax.nn.silu(pre_act).astype(jnp.bfloat16)
    embedding = jnp.dot(hidden, w_out, preferred_element_type=jnp.float32)
    spread = jnp.sqrt(jnp.mean(embedding * embedding, axis=1, keepdims=True) + EPSILON)
    unit_rows = (embedding / spread).astype(jnp.bfloat16)
    return (pre_act, hidden, embedding, spread, unit_rows)


def rows_of(index, count=TILE):
    return pl.ds(pl.multiple_of(index * count, count), count)


def pick_kernel(asked_ref, table_ref, out_ref):
    def step(slot, carry):
        out_ref[rows_of(slot), :] = table_ref[rows_of(asked_ref[slot]), :]
        return carry

    lax.fori_loop(0, out_ref.shape[0] // TILE, step, 0, unroll=2)


def pick_tiles(asked, table, slots):
    shape = (slots * TILE, table.shape[1])
    return pl.pallas_call(
        pick_kernel,
        out_shape=jax.ShapeDtypeStruct(shape, table.dtype),
        grid_spec=pltpu.PrefetchScalarGridSpec(
            num_scalar_prefetch=1,
            grid=(1,),
            in_specs=[whole(table.shape)],
            out_specs=whole(shape),
        ),
        compiler_params=pltpu.CompilerParams(vmem_limit_bytes=VMEM_LIMIT),
    )(asked, table)


def score_kernel(
    local_count,
    remote_count,
    slot_count,
    lanes,
    ids_ref,
    tiles_ref,
    refs_ref,
    counts_ref,
    table_ref,
    fetched_ref,
    teacher_ref,
    kl_ref,
    local_grad_ref,
    remote_grad_ref,
    table_f,
    remote_acc,
    context,
    delta,
    anchor_rows,
    anchor_grad,
    *row_accs,
):
    block = pl.program_id(0)
    width = table_ref.shape[1]
    scale = SCORE_SCALE / width
    zero_chunk = jnp.zeros((CHUNK, width), jnp.float32)

    @pl.when(block == 0)
    def _():
        def clear(index, carry):
            here = rows_of(index, CHUNK)
            table_f[here, :] = table_ref[here, :].astype(jnp.float32)
            local_grad_ref[here, :] = zero_chunk
            for acc in row_accs:
                acc[here, :] = zero_chunk
            return carry

        lax.fori_loop(0, table_f.shape[0] // CHUNK, clear, 0)

        def clear_remote(index, carry):
            remote_acc[rows_of(index, CHUNK), :] = zero_chunk
            return carry

        lax.fori_loop(0, remote_acc.shape[0] // CHUNK, clear_remote, 0)

    rows = [ids_ref[block * ABLK + row] for row in range(ABLK)]
    for row in range(ABLK):
        anchor_rows[row : row + 1, :] = table_f[pl.ds(rows[row], 1), :]
    anchors = (anchor_rows[...] * scale).astype(jnp.bfloat16)

    places = []
    lives = []
    for i in range(local_count):
        place = rows_of(tiles_ref[block * local_count + i])
        context[i * TILE : (i + 1) * TILE, :] = table_ref[place, :]
        places.append(place)
        lives.append(None)
    for i in range(remote_count):
        ref = refs_ref[block * remote_count + i]
        place = rows_of(ref)
        at = local_count + i
        context[at * TILE : (at + 1) * TILE, :] = fetched_ref[place, :]
        places.append(place)
        live = lax.rem(ref, slot_count) < counts_ref[lax.div(ref, slot_count)]
        lives.append(jnp.where(live, 1.0, 0.0).astype(jnp.float32))

    student = []
    target = []
    student_sum = target_sum = gap_sum = None
    for i in range(local_count + remote_count):
        span = slice(i * TILE, (i + 1) * TILE)
        scores = lax.dot_general(
            anchors,
            context[span, :],
            (((1,), (1,)), ((), ())),
            preferred_element_type=jnp.float32,
        )
        teacher = teacher_ref[:, span].astype(jnp.float32)
        student_exp = jnp.exp(scores)
        target_exp = jnp.exp(teacher)
        if lives[i] is not None:
            student_exp = student_exp * lives[i]
            target_exp = target_exp * lives[i]
        gap = target_exp * (teacher - scores)
        student_sum = student_exp if i == 0 else student_sum + student_exp
        target_sum = target_exp if i == 0 else target_sum + target_exp
        gap_sum = gap if i == 0 else gap_sum + gap
        student.append(student_exp)
        target.append(target_exp)
    student_total = jnp.sum(student_sum, axis=1, keepdims=True)
    target_total = jnp.sum(target_sum, axis=1, keepdims=True)
    gap_total = jnp.sum(gap_sum, axis=1, keepdims=True)
    student_inv = 1.0 / student_total
    target_inv = 1.0 / target_total
    divergence = gap_total * target_inv - jnp.log(target_total) + jnp.log(student_total)
    kl_ref[0] = jnp.broadcast_to(divergence, (ABLK, TILE)).T[0:1, :]
    for i in range(local_count + remote_count):
        span = slice(i * TILE, (i + 1) * TILE)
        delta[:, span] = (student[i] * student_inv - target[i] * target_inv).astype(jnp.bfloat16)
    anchor_grad[...] = (
        jnp.dot(delta[...], context[...], preferred_element_type=jnp.float32) * scale
    )
    for i in range(local_count + remote_count):
        span = slice(i * TILE, (i + 1) * TILE)
        context_grad = lax.dot_general(
            delta[:, span],
            anchors,
            (((0,), (0,)), ((), ())),
            preferred_element_type=jnp.float32,
        )
        acc = local_grad_ref if i < local_count else remote_acc
        acc[places[i], :] += context_grad
    for row in range(ABLK):
        acc = row_accs[row % lanes]
        acc[pl.ds(rows[row], 1), :] += anchor_grad[row : row + 1, :]

    @pl.when(block == pl.num_programs(0) - 1)
    def _():
        def finish(index, carry):
            here = rows_of(index, CHUNK)
            total = local_grad_ref[here, :]
            for acc in row_accs:
                total = total + acc[here, :]
            local_grad_ref[here, :] = total
            return carry

        lax.fori_loop(0, table_f.shape[0] // CHUNK, finish, 0)

        def finish_remote(index, carry):
            here = rows_of(index, CHUNK)
            remote_grad_ref[here, :] = remote_acc[here, :].astype(jnp.bfloat16)
            return carry

        lax.fori_loop(0, remote_acc.shape[0] // CHUNK, finish_remote, 0)


def score(anchor_ids, local_tiles, remote_refs, own_counts, table, fetched, teacher, slot_count):
    blocks, local_count = local_tiles.shape
    remote_count = remote_refs.shape[1]
    context_width = teacher.shape[1]
    width = table.shape[1]
    lanes = 4 if table.shape[0] <= 8192 else 1
    kernel = functools.partial(score_kernel, local_count, remote_count, slot_count, lanes)
    kl, local_grad, remote_grad = pl.pallas_call(
        kernel,
        out_shape=(
            jax.ShapeDtypeStruct((blocks, 1, ABLK), jnp.float32),
            jax.ShapeDtypeStruct(table.shape, jnp.float32),
            jax.ShapeDtypeStruct(fetched.shape, jnp.bfloat16),
        ),
        grid_spec=pltpu.PrefetchScalarGridSpec(
            num_scalar_prefetch=4,
            grid=(blocks,),
            in_specs=[
                whole(table.shape),
                whole(fetched.shape),
                pl.BlockSpec((ABLK, context_width), lambda b, *_: (b, 0)),
            ],
            out_specs=(
                pl.BlockSpec((1, 1, ABLK), lambda b, *_: (b, 0, 0)),
                whole(table.shape),
                whole(fetched.shape),
            ),
            scratch_shapes=[
                pltpu.VMEM(table.shape, jnp.float32),
                pltpu.VMEM(fetched.shape, jnp.float32),
                pltpu.VMEM((context_width, width), jnp.bfloat16),
                pltpu.VMEM((ABLK, context_width), jnp.bfloat16),
                pltpu.VMEM((ABLK, width), jnp.float32),
                pltpu.VMEM((ABLK, width), jnp.float32),
            ]
            + [pltpu.VMEM(table.shape, jnp.float32)] * lanes,
        ),
        compiler_params=pltpu.CompilerParams(vmem_limit_bytes=VMEM_LIMIT),
    )(
        anchor_ids,
        local_tiles.reshape(-1),
        remote_refs.reshape(-1),
        own_counts,
        table,
        fetched,
        teacher,
    )
    return kl.reshape(-1), local_grad, remote_grad


def merge_kernel(asked_ref, local_ref, returned_ref, out_ref, acc):
    def load(index, carry):
        here = rows_of(index, CHUNK)
        acc[here, :] = local_ref[here, :]
        return carry

    lax.fori_loop(0, acc.shape[0] // CHUNK, load, 0)

    def add(slot, carry):
        acc[rows_of(asked_ref[slot]), :] += returned_ref[rows_of(slot), :].astype(jnp.float32)
        return carry

    lax.fori_loop(0, returned_ref.shape[0] // TILE, add, 0)

    def store(index, carry):
        here = rows_of(index, CHUNK)
        out_ref[here, :] = acc[here, :].astype(jnp.bfloat16)
        return carry

    lax.fori_loop(0, acc.shape[0] // CHUNK, store, 0)


def merge(asked, local_grad, returned):
    return pl.pallas_call(
        merge_kernel,
        out_shape=jax.ShapeDtypeStruct(local_grad.shape, jnp.bfloat16),
        grid_spec=pltpu.PrefetchScalarGridSpec(
            num_scalar_prefetch=1,
            grid=(1,),
            in_specs=[whole(local_grad.shape), whole(returned.shape)],
            out_specs=whole(local_grad.shape),
            scratch_shapes=[pltpu.VMEM(local_grad.shape, jnp.float32)],
        ),
        compiler_params=pltpu.CompilerParams(vmem_limit_bytes=VMEM_LIMIT),
    )(asked, local_grad, returned)


MESH = pl.DeviceIdType.MESH
ANYWHERE = pl.BlockSpec(memory_space=pl.ANY)
IN_VMEM = pl.BlockSpec(memory_space=pltpu.VMEM)


def greet(partners):
    barrier = pltpu.get_barrier_semaphore()
    for partner in partners:
        pl.semaphore_signal(barrier, inc=1, device_id=partner, device_id_type=MESH)
    pl.semaphore_wait(barrier, len(partners))


def push(src, dst, sems, index, partner):
    copy = pltpu.make_async_remote_copy(
        src_ref=src,
        dst_ref=dst,
        send_sem=sems[0].at[index],
        recv_sem=sems[1].at[index],
        device_id=partner,
        device_id_type=MESH,
    )
    copy.start()
    return copy


def dom_partners(doms):
    group, dom = lax.axis_index("group"), lax.axis_index("dom")
    chips = doms // 2
    chip, core = dom // 2, dom % 2
    other = chip * 2 + (1 - core)
    ahead = [lax.rem(chip + k, chips) * 2 + core for k in range(1, chips)]
    behind = [lax.rem(chip + chips - k, chips) for k in range(1, chips)]
    return group, dom, core, other, ahead, behind


def gather_kernel(
    groups, doms, unit_ref, requests_ref, table_ref, asked_ref,
    own_sem, near_send, near_recv, far_send, far_recv, on_send, on_recv, ask_send, ask_recv,
):
    group, dom, core, other, ahead, behind = dom_partners(doms)
    count = unit_ref.shape[0]
    peers = [lax.rem(group + k, groups) for k in range(1, groups)]
    greet([(group, other)] + [(group, far) for far in ahead] + [(peer, dom) for peer in peers])
    here = table_ref.at[rows_of(dom, count), :]
    far_copies = [
        push(unit_ref, here, (far_send, far_recv), k, (group, far)) for k, far in enumerate(ahead)
    ]
    ask_copies = [
        push(requests_ref.at[peer], asked_ref.at[group], (ask_send, ask_recv), k, (peer, dom))
        for k, peer in enumerate(peers)
    ]
    near = push(unit_ref, here, (near_send, near_recv), 0, (group, other))
    own = pltpu.make_async_copy(unit_ref, here, own_sem.at[0])
    own.start()
    own_ask = pltpu.make_async_copy(requests_ref.at[group], asked_ref.at[group], own_sem.at[1])
    own_ask.start()
    on_copies = []
    for k, copy in enumerate(far_copies):
        copy.wait_recv()
        block = table_ref.at[rows_of(behind[k] * 2 + core, count), :]
        on_copies.append(push(block, block, (on_send, on_recv), k, (group, other)))
    own.wait()
    own_ask.wait()
    near.wait()
    for copy in ask_copies:
        copy.wait()
    for copy in far_copies:
        copy.wait_send()
    for copy in on_copies:
        copy.wait()


def gather_table(unit_rows, own_requests, groups, doms):
    slots = own_requests.shape[1]
    asks = jnp.broadcast_to(own_requests[:, None, :], (groups, 8, slots))
    asks = jnp.pad(asks, ((0, 0), (0, 0), (0, 128 - slots)))
    far, peers = max(doms // 2 - 1, 1), max(groups - 1, 1)
    dma = pltpu.SemaphoreType.DMA
    table, asked = pl.pallas_call(
        functools.partial(gather_kernel, groups, doms),
        out_shape=(
            jax.ShapeDtypeStruct((doms * unit_rows.shape[0], unit_rows.shape[1]), unit_rows.dtype),
            jax.ShapeDtypeStruct(asks.shape, asks.dtype),
        ),
        in_specs=[ANYWHERE, ANYWHERE],
        out_specs=(ANYWHERE, ANYWHERE),
        scratch_shapes=[
            dma((2,)), dma((1,)), dma((1,)), dma((far,)), dma((far,)),
            dma((far,)), dma((far,)), dma((peers,)), dma((peers,)),
        ],
        compiler_params=pltpu.CompilerParams(collective_id=0, has_side_effects=True),
    )(unit_rows, asks)
    return table, asked[:, 0, :slots].reshape(-1)


def scatter_kernel(
    doms, merged_ref, out_ref, mine, kept, near_got, far_out, far_got,
    own_sem, near_send, near_recv, far_send, far_recv,
):
    group, dom, core, other, ahead, behind = dom_partners(doms)
    count = out_ref.shape[0]
    chips = doms // 2
    greet([(group, other)] + [(group, far) for far in ahead])
    order = [dom // 2] + [lax.rem(dom // 2 + k, chips) for k in range(1, chips)]
    order = order[1:] + order[:1]
    near_copies = []
    own_copies = []
    for k, chip in enumerate(order):
        theirs = merged_ref.at[rows_of(chip * 2 + (1 - core), count), :]
        near_copies.append(push(theirs, near_got.at[k], (near_send, near_recv), k, (group, other)))
        ours = merged_ref.at[rows_of(chip * 2 + core, count), :]
        copy = pltpu.make_async_copy(ours, mine.at[k], own_sem.at[k])
        copy.start()
        own_copies.append(copy)
    far_copies = []
    for k in range(chips - 1):
        near_copies[k].wait_recv()
        own_copies[k].wait()
        total = mine[k].astype(jnp.float32) + near_got[k].astype(jnp.float32)
        far_out[k] = total.astype(jnp.bfloat16)
        far_copies.append(
            push(far_out.at[k], far_got.at[k], (far_send, far_recv), k, (group, ahead[k]))
        )
    near_copies[chips - 1].wait_recv()
    own_copies[chips - 1].wait()
    kept[...] = mine[chips - 1].astype(jnp.float32) + near_got[chips - 1].astype(jnp.float32)
    for k, copy in enumerate(far_copies):
        copy.wait_recv()
        kept[...] += far_got[k].astype(jnp.float32)
    out_ref[...] = kept[...]
    for copy in near_copies + far_copies:
        copy.wait_send()


def scatter_sums(merged, doms):
    count, width = merged.shape[0] // doms, merged.shape[1]
    chips = doms // 2
    far = max(chips - 1, 1)
    dma = pltpu.SemaphoreType.DMA
    return pl.pallas_call(
        functools.partial(scatter_kernel, doms),
        out_shape=jax.ShapeDtypeStruct((count, width), jnp.float32),
        in_specs=[ANYWHERE],
        out_specs=IN_VMEM,
        scratch_shapes=[
            pltpu.VMEM((chips, count, width), jnp.bfloat16),
            pltpu.VMEM((count, width), jnp.float32),
            pltpu.VMEM((chips, count, width), jnp.bfloat16),
            pltpu.VMEM((far, count, width), jnp.bfloat16),
            pltpu.VMEM((far, count, width), jnp.bfloat16),
            dma((chips,)), dma((chips,)), dma((chips,)), dma((far,)), dma((far,)),
        ],
        compiler_params=pltpu.CompilerParams(
            collective_id=1, has_side_effects=True, vmem_limit_bytes=VMEM_LIMIT
        ),
    )(merged)


def totals_kernel(
    groups, doms, x_ref, out_ref, out1, got1, part, out2, got2, gather1, gather2,
    send1, recv1, send2, recv2, send3, recv3, send4, recv4,
):
    group, dom = lax.axis_index("group"), lax.axis_index("dom")
    wide = x_ref.shape[0] // doms
    thin = wide // groups
    dom_peers = [lax.rem(dom + k, doms) for k in range(1, doms)]
    group_peers = [lax.rem(group + k, groups) for k in range(1, groups)]
    greet([(group, peer) for peer in dom_peers] + [(peer, dom) for peer in group_peers])
    copies = []
    first = []
    for k, peer in enumerate(dom_peers):
        out1[k] = x_ref[rows_of(peer, wide), :].astype(jnp.bfloat16)
        first.append(push(out1.at[k], got1.at[k], (send1, recv1), k, (group, peer)))
    part[...] = x_ref[rows_of(dom, wide), :]
    for k, copy in enumerate(first):
        copy.wait_recv()
        part[...] += got1[k].astype(jnp.float32)
    copies += first
    second = []
    for k, peer in enumerate(group_peers):
        out2[k] = part[rows_of(peer, thin), :].astype(jnp.bfloat16)
        second.append(push(out2.at[k], got2.at[k], (send2, recv2), k, (peer, dom)))
    total = part[rows_of(group, thin), :]
    for k, copy in enumerate(second):
        copy.wait_recv()
        total = total + got2[k].astype(jnp.float32)
    copies += second
    gather1[group] = (total * (1.0 / (groups * doms))).astype(jnp.bfloat16)
    mine = gather1.at[group]
    third = [
        push(mine, mine, (send3, recv3), k, (peer, dom)) for k, peer in enumerate(group_peers)
    ]
    for copy in third:
        copy.wait_recv()
    copies += third
    fourth = [
        push(gather1, gather2.at[dom], (send4, recv4), k, (group, peer))
        for k, peer in enumerate(dom_peers)
    ]
    out_ref[dom] = gather1[...].astype(jnp.float32)
    for k, copy in enumerate(fourth):
        copy.wait_recv()
        source = lax.rem(dom + doms - (k + 1), doms)
        out_ref[source] = gather2[source].astype(jnp.float32)
    copies += fourth
    for copy in copies:
        copy.wait_send()


def mean_over_devices(x, groups, doms):
    rows, width = x.shape
    wide = rows // doms
    thin = wide // groups
    a, b = max(doms - 1, 1), max(groups - 1, 1)
    half = jnp.bfloat16
    dma = pltpu.SemaphoreType.DMA
    out = pl.pallas_call(
        functools.partial(totals_kernel, groups, doms),
        out_shape=jax.ShapeDtypeStruct((doms, groups, thin, width), jnp.float32),
        in_specs=[IN_VMEM],
        out_specs=IN_VMEM,
        scratch_shapes=[
            pltpu.VMEM((a, wide, width), half),
            pltpu.VMEM((a, wide, width), half),
            pltpu.VMEM((wide, width), jnp.float32),
            pltpu.VMEM((b, thin, width), half),
            pltpu.VMEM((b, thin, width), half),
            pltpu.VMEM((groups, thin, width), half),
            pltpu.VMEM((doms, groups, thin, width), half),
            dma((a,)), dma((a,)), dma((b,)), dma((b,)), dma((b,)), dma((b,)), dma((a,)), dma((a,)),
        ],
        compiler_params=pltpu.CompilerParams(
            collective_id=2, has_side_effects=True, vmem_limit_bytes=VMEM_LIMIT
        ),
    )(x)
    return out.reshape(rows, width)


def shards(
    features, w_in, b_in, w_out, anchor_ids, local_tiles, requests, counts, remote_refs, teacher
):
    groups = lax.axis_size("group")
    doms = lax.axis_size("dom")
    devices = groups * doms
    own_requests = requests[0, 0]
    own_counts = counts[0, 0]
    slot_count = own_requests.shape[1]
    pre_act, hidden, embedding, spread, unit_rows = node_forward(features, w_in, b_in, w_out)
    table, asked = gather_table(unit_rows, own_requests, groups, doms)
    served = pick_tiles(asked, table, groups * slot_count)
    fetched = lax.all_to_all(served, "group", split_axis=0, concat_axis=0, tiled=True)
    anchor_kl, local_grad, remote_grad = score(
        anchor_ids, local_tiles, remote_refs, own_counts, table, fetched, teacher, slot_count
    )
    returned = lax.all_to_all(remote_grad, "group", split_axis=0, concat_axis=0, tiled=True)
    merged = merge(asked, local_grad, returned)
    node_grad = scatter_sums(merged, doms)
    normed = embedding / spread
    embed_grad = (
        (node_grad - normed * jnp.mean(node_grad * normed, axis=1, keepdims=True)) / spread
    ).astype(jnp.bfloat16)
    out_grad = jnp.dot(hidden.T, embed_grad, preferred_element_type=jnp.float32)
    hidden_grad = jnp.dot(embed_grad, w_out.T, preferred_element_type=jnp.float32)
    sigmoid_pre = jax.nn.sigmoid(pre_act)
    pre_grad = hidden_grad * sigmoid_pre * (1.0 + pre_act * (1.0 - sigmoid_pre))
    bias_grad = jnp.sum(pre_grad, axis=0)
    in_grad_t = jnp.dot(
        pre_grad.astype(jnp.bfloat16).T, features, preferred_element_type=jnp.float32
    )
    hid = in_grad_t.shape[0]
    width = out_grad.shape[1]
    bias_rows = bias_grad.reshape(-1, width)
    used = 2 * hid + bias_rows.shape[0]
    unit = devices * 16
    padding = -used % unit
    stacked = jnp.concatenate(
        [in_grad_t, out_grad, bias_rows, jnp.zeros((padding, width), jnp.float32)], axis=0
    )
    totals = mean_over_devices(stacked, groups, doms)
    return (
        anchor_kl,
        node_grad,
        totals[:hid].T,
        totals[2 * hid : used].reshape(-1),
        totals[hid : 2 * hid],
    )


def solution(mesh):
    return jax.shard_map(
        shards,
        mesh=mesh,
        in_specs=(
            P(("group", "dom"), None),
            P(),
            P(),
            P(),
            P(("group", "dom")),
            P(("group", "dom"), None),
            P("group", "dom", None, None),
            P("group", "dom", None),
            P(("group", "dom"), None),
            P(("group", "dom"), None),
        ),
        out_specs=(P(("group", "dom")), P(("group", "dom"), None), P(), P(), P()),
        check_vma=False,
    )
```

```python
import functools
import math

import jax
import jax.numpy as jnp
from jax import lax
from jax.experimental import pallas as pl
from jax.experimental.pallas import tpu as pltpu
from jax.sharding import PartitionSpec as P

TILE = 128
ABLK = 128

SCORE_SCALE = 8.0
EPSILON = 1e-06
VMEM_LIMIT = 60 * 1024 * 1024
CHUNK = 256

ONE_COPY = pl.Buffered(1)


def whole(shape):
    return pl.BlockSpec(shape, lambda *_: (0,) * len(shape), pipeline_mode=ONE_COPY)


def node_forward(feature_rows, w_in, b_in, w_out):
    pre_act = jnp.dot(feature_rows, w_in, preferred_element_type=jnp.float32) + b_in
    hidden = jax.nn.silu(pre_act).astype(jnp.bfloat16)
    embedding = jnp.dot(hidden, w_out, preferred_element_type=jnp.float32)
    spread = jnp.sqrt(jnp.mean(embedding * embedding, axis=1, keepdims=True) + EPSILON)
    unit_rows = (embedding / spread).astype(jnp.bfloat16)
    return (pre_act, hidden, embedding, spread, unit_rows)


def rows_of(index, count=TILE):
    return pl.ds(pl.multiple_of(index * count, count), count)


def pick_kernel(asked_ref, table_ref, out_ref):
    def step(slot, carry):
        out_ref[rows_of(slot), :] = table_ref[rows_of(asked_ref[slot]), :]
        return carry

    lax.fori_loop(0, out_ref.shape[0] // TILE, step, 0, unroll=2)


def pick_tiles(asked, table, slots):
    shape = (slots * TILE, table.shape[1])
    return pl.pallas_call(
        pick_kernel,
        out_shape=jax.ShapeDtypeStruct(shape, table.dtype),
        grid_spec=pltpu.PrefetchScalarGridSpec(
            num_scalar_prefetch=1,
            grid=(1,),
            in_specs=[whole(table.shape)],
            out_specs=whole(shape),
        ),
        compiler_params=pltpu.CompilerParams(vmem_limit_bytes=VMEM_LIMIT),
    )(asked, table)


def cost(flops, moved, powers):
    return pl.CostEstimate(flops=flops, bytes_accessed=moved, transcendentals=powers)


def clear_rows(ref):
    zero_chunk = jnp.zeros((CHUNK, ref.shape[1]), ref.dtype)

    def clear(index, carry):
        ref[rows_of(index, CHUNK), :] = zero_chunk
        return carry

    lax.fori_loop(0, ref.shape[0] // CHUNK, clear, 0)


def as_row(column):
    return jnp.broadcast_to(column, (ABLK, TILE)).T[0:1, :]


def prepare_kernel(
    per_step, local_count, remote_count, slot_count, ids_ref, refs_ref, counts_ref,
    table_ref, teacher_ref, anchors_ref, target_ref, base_ref, table_f, anchor_rows,
):
    scale = SCORE_SCALE / table_ref.shape[1]

    @pl.when(pl.program_id(0) == 0)
    def _():
        def widen(index, carry):
            here = rows_of(index, CHUNK)
            table_f[here, :] = table_ref[here, :].astype(jnp.float32)
            return carry

        lax.fori_loop(0, table_f.shape[0] // CHUNK, widen, 0)

    for sub in range(per_step):
        block = pl.program_id(0) * per_step + sub
        rows = slice(sub * ABLK, (sub + 1) * ABLK)
        for row in range(ABLK):
            at = sub * ABLK + row
            index = ids_ref[block * ABLK + row]
            anchor_rows[at : at + 1, :] = table_f[pl.ds(index, 1), :]
        target_sum = gap_sum = None
        exps = []
        for i in range(local_count + remote_count):
            teacher = teacher_ref[rows, i * TILE : (i + 1) * TILE].astype(jnp.float32)
            target_exp = jnp.exp(teacher)
            if i >= local_count:
                ref = refs_ref[block * remote_count + i - local_count]
                live = lax.rem(ref, slot_count) < counts_ref[lax.div(ref, slot_count)]
                target_exp = target_exp * jnp.where(live, 1.0, 0.0).astype(jnp.float32)
            gap = target_exp * teacher
            target_sum = target_exp if i == 0 else target_sum + target_exp
            gap_sum = gap if i == 0 else gap_sum + gap
            exps.append(target_exp)
        total = jnp.sum(target_sum, axis=1, keepdims=True)
        inverse = 1.0 / total
        base = jnp.sum(gap_sum, axis=1, keepdims=True) * inverse - jnp.log(total)
        base_ref[sub] = as_row(base)
        for i, target_exp in enumerate(exps):
            target_ref[rows, i * TILE : (i + 1) * TILE] = (target_exp * inverse).astype(
                jnp.bfloat16
            )
    anchors_ref[...] = (anchor_rows[...] * scale).astype(jnp.bfloat16)


def prepare(per_step, anchor_ids, remote_refs, local_count, own_counts, table, teacher, slots):
    blocks, remote_count = remote_refs.shape
    anchors, context_width = teacher.shape
    width = table.shape[1]
    rows = per_step * ABLK
    return pl.pallas_call(
        functools.partial(prepare_kernel, per_step, local_count, remote_count, slots),
        out_shape=(
            jax.ShapeDtypeStruct((anchors, width), jnp.bfloat16),
            jax.ShapeDtypeStruct((anchors, context_width), jnp.bfloat16),
            jax.ShapeDtypeStruct((blocks, 1, ABLK), jnp.float32),
        ),
        grid_spec=pltpu.PrefetchScalarGridSpec(
            num_scalar_prefetch=3,
            grid=(blocks // per_step,),
            in_specs=[
                whole(table.shape),
                pl.BlockSpec((rows, context_width), lambda b, *_: (b, 0)),
            ],
            out_specs=(
                pl.BlockSpec((rows, width), lambda b, *_: (b, 0)),
                pl.BlockSpec((rows, context_width), lambda b, *_: (b, 0)),
                pl.BlockSpec((per_step, 1, ABLK), lambda b, *_: (b, 0, 0)),
            ),
            scratch_shapes=[
                pltpu.VMEM(table.shape, jnp.float32),
                pltpu.VMEM((rows, width), jnp.float32),
            ],
        ),
        compiler_params=pltpu.CompilerParams(vmem_limit_bytes=VMEM_LIMIT),
        cost_estimate=cost(
            10 * anchors * context_width, 4 * anchors * context_width, anchors * context_width
        ),
    )(anchor_ids, remote_refs.reshape(-1), own_counts, table, teacher)


def take_context(block, sub, context, tiles_ref, refs_ref, table_ref, fetched_ref, counts):
    local_count, remote_count = counts
    places = []
    for i in range(local_count):
        place = rows_of(tiles_ref[block * local_count + i])
        context[sub, i * TILE : (i + 1) * TILE, :] = table_ref[place, :]
        places.append(place)
    for i in range(remote_count):
        place = rows_of(refs_ref[block * remote_count + i])
        at = local_count + i
        context[sub, at * TILE : (at + 1) * TILE, :] = fetched_ref[place, :]
        places.append(place)
    return places


def tile_grad(delta, anchors):
    return lax.dot_general(
        delta, anchors, (((0,), (0,)), ((), ())), preferred_element_type=jnp.float32
    )


def score_kernel(
    per_step, local_count, remote_count, slot_count, tiles_ref, refs_ref, counts_ref,
    table_ref, fetched_ref, anchors_ref, target_ref, base_ref,
    kl_ref, delta_ref, remote_grad_ref, remote_acc, context,
):
    tiles = local_count + remote_count

    @pl.when(pl.program_id(0) == 0)
    def _():
        clear_rows(remote_acc)

    for sub in range(per_step):
        block = pl.program_id(0) * per_step + sub
        rows = slice(sub * ABLK, (sub + 1) * ABLK)
        places = take_context(
            block, sub, context, tiles_ref, refs_ref, table_ref, fetched_ref,
            (local_count, remote_count),
        )
        anchors = anchors_ref[rows, :]
        student = []
        student_sum = gap_sum = None
        for i in range(tiles):
            span = slice(i * TILE, (i + 1) * TILE)
            scores = lax.dot_general(
                anchors,
                context[sub, span, :],
                (((1,), (1,)), ((), ())),
                preferred_element_type=jnp.float32,
            )
            student_exp = jnp.exp(scores)
            if i >= local_count:
                ref = refs_ref[block * remote_count + i - local_count]
                live = lax.rem(ref, slot_count) < counts_ref[lax.div(ref, slot_count)]
                student_exp = student_exp * jnp.where(live, 1.0, 0.0).astype(jnp.float32)
            gap = target_ref[rows, span].astype(jnp.float32) * scores
            student_sum = student_exp if i == 0 else student_sum + student_exp
            gap_sum = gap if i == 0 else gap_sum + gap
            student.append(student_exp)
        total = jnp.sum(student_sum, axis=1, keepdims=True)
        inverse = 1.0 / total
        rest = jnp.log(total) - jnp.sum(gap_sum, axis=1, keepdims=True)
        kl_ref[sub] = base_ref[sub] + as_row(rest)
        for i in range(tiles):
            span = slice(i * TILE, (i + 1) * TILE)
            delta = (student[i] * inverse - target_ref[rows, span].astype(jnp.float32)).astype(
                jnp.bfloat16
            )
            delta_ref[rows, span] = delta
            if i >= local_count:
                remote_acc[places[i], :] += tile_grad(delta, anchors)

    @pl.when(pl.program_id(0) == pl.num_programs(0) - 1)
    def _():
        def finish(index, carry):
            here = rows_of(index, CHUNK)
            remote_grad_ref[here, :] = remote_acc[here, :].astype(jnp.bfloat16)
            return carry

        lax.fori_loop(0, remote_acc.shape[0] // CHUNK, finish, 0)


def score(per_step, local_tiles, remote_refs, own_counts, table, fetched, prepared, slots):
    anchors, target, base = prepared
    blocks, local_count = local_tiles.shape
    remote_count = remote_refs.shape[1]
    context_width = target.shape[1]
    width = table.shape[1]
    rows = per_step * ABLK
    pairs = target.shape[0] * context_width
    return pl.pallas_call(
        functools.partial(score_kernel, per_step, local_count, remote_count, slots),
        out_shape=(
            jax.ShapeDtypeStruct((blocks, 1, ABLK), jnp.float32),
            jax.ShapeDtypeStruct(target.shape, jnp.bfloat16),
            jax.ShapeDtypeStruct(fetched.shape, jnp.bfloat16),
        ),
        grid_spec=pltpu.PrefetchScalarGridSpec(
            num_scalar_prefetch=3,
            grid=(blocks // per_step,),
            in_specs=[
                whole(table.shape),
                whole(fetched.shape),
                pl.BlockSpec((rows, width), lambda b, *_: (b, 0)),
                pl.BlockSpec((rows, context_width), lambda b, *_: (b, 0)),
                pl.BlockSpec((per_step, 1, ABLK), lambda b, *_: (b, 0, 0)),
            ],
            out_specs=(
                pl.BlockSpec((per_step, 1, ABLK), lambda b, *_: (b, 0, 0)),
                pl.BlockSpec((rows, context_width), lambda b, *_: (b, 0)),
                whole(fetched.shape),
            ),
            scratch_shapes=[
                pltpu.VMEM(fetched.shape, jnp.float32),
                pltpu.VMEM((per_step, context_width, width), jnp.bfloat16),
            ],
        ),
        compiler_params=pltpu.CompilerParams(vmem_limit_bytes=VMEM_LIMIT),
        cost_estimate=cost(3 * pairs * width, 4 * pairs, pairs),
    )(
        local_tiles.reshape(-1), remote_refs.reshape(-1), own_counts,
        table, fetched, anchors, target, base,
    )


def local_kernel(
    per_step, local_count, remote_count, lanes, ids_ref, tiles_ref, refs_ref,
    table_ref, fetched_ref, anchors_ref, delta_ref, local_grad_ref,
    context, anchor_grad, *row_accs,
):
    scale = SCORE_SCALE / table_ref.shape[1]

    @pl.when(pl.program_id(0) == 0)
    def _():
        clear_rows(local_grad_ref)
        for acc in row_accs:
            clear_rows(acc)

    for sub in range(per_step):
        block = pl.program_id(0) * per_step + sub
        rows = slice(sub * ABLK, (sub + 1) * ABLK)
        places = take_context(
            block, sub, context, tiles_ref, refs_ref, table_ref, fetched_ref,
            (local_count, remote_count),
        )
        anchor_grad[rows, :] = (
            jnp.dot(delta_ref[rows, :], context[sub], preferred_element_type=jnp.float32) * scale
        )
        anchors = anchors_ref[rows, :]
        for i in range(local_count):
            span = slice(i * TILE, (i + 1) * TILE)
            local_grad_ref[places[i], :] += tile_grad(delta_ref[rows, span], anchors)
        for row in range(ABLK):
            acc = row_accs[row % lanes]
            at = sub * ABLK + row
            acc[pl.ds(ids_ref[block * ABLK + row], 1), :] += anchor_grad[at : at + 1, :]

    @pl.when(pl.program_id(0) == pl.num_programs(0) - 1)
    def _():
        def finish(index, carry):
            here = rows_of(index, CHUNK)
            total = local_grad_ref[here, :]
            for acc in row_accs:
                total = total + acc[here, :]
            local_grad_ref[here, :] = total
            return carry

        lax.fori_loop(0, local_grad_ref.shape[0] // CHUNK, finish, 0)


def local_grads(per_step, anchor_ids, local_tiles, remote_refs, table, fetched, anchors, delta):
    blocks, local_count = local_tiles.shape
    remote_count = remote_refs.shape[1]
    context_width = delta.shape[1]
    width = table.shape[1]
    rows = per_step * ABLK
    lanes = 4 if table.shape[0] <= 8192 else 1
    pairs = delta.shape[0] * context_width
    return pl.pallas_call(
        functools.partial(local_kernel, per_step, local_count, remote_count, lanes),
        out_shape=jax.ShapeDtypeStruct(table.shape, jnp.float32),
        grid_spec=pltpu.PrefetchScalarGridSpec(
            num_scalar_prefetch=3,
            grid=(blocks // per_step,),
            in_specs=[
                whole(table.shape),
                whole(fetched.shape),
                pl.BlockSpec((rows, width), lambda b, *_: (b, 0)),
                pl.BlockSpec((rows, context_width), lambda b, *_: (b, 0)),
            ],
            out_specs=whole(table.shape),
            scratch_shapes=[
                pltpu.VMEM((per_step, context_width, width), jnp.bfloat16),
                pltpu.VMEM((rows, width), jnp.float32),
            ]
            + [pltpu.VMEM(table.shape, jnp.float32)] * lanes,
        ),
        compiler_params=pltpu.CompilerParams(vmem_limit_bytes=VMEM_LIMIT),
        cost_estimate=cost(3 * pairs * width, 2 * pairs, 0),
    )(
        anchor_ids, local_tiles.reshape(-1), remote_refs.reshape(-1),
        table, fetched, anchors, delta,
    )


def merge_kernel(asked_ref, local_ref, returned_ref, out_ref, acc):
    def load(index, carry):
        here = rows_of(index, CHUNK)
        acc[here, :] = local_ref[here, :]
        return carry

    lax.fori_loop(0, acc.shape[0] // CHUNK, load, 0)

    def add(slot, carry):
        acc[rows_of(asked_ref[slot]), :] += returned_ref[rows_of(slot), :].astype(jnp.float32)
        return carry

    lax.fori_loop(0, returned_ref.shape[0] // TILE, add, 0)

    def store(index, carry):
        here = rows_of(index, CHUNK)
        out_ref[here, :] = acc[here, :].astype(jnp.bfloat16)
        return carry

    lax.fori_loop(0, acc.shape[0] // CHUNK, store, 0)


def merge(asked, local_grad, returned):
    return pl.pallas_call(
        merge_kernel,
        out_shape=jax.ShapeDtypeStruct(local_grad.shape, jnp.bfloat16),
        grid_spec=pltpu.PrefetchScalarGridSpec(
            num_scalar_prefetch=1,
            grid=(1,),
            in_specs=[whole(local_grad.shape), whole(returned.shape)],
            out_specs=whole(local_grad.shape),
            scratch_shapes=[pltpu.VMEM(local_grad.shape, jnp.float32)],
        ),
        compiler_params=pltpu.CompilerParams(vmem_limit_bytes=VMEM_LIMIT),
    )(asked, local_grad, returned)


MESH = pl.DeviceIdType.MESH
ANYWHERE = pl.BlockSpec(memory_space=pl.ANY)
IN_VMEM = pl.BlockSpec(memory_space=pltpu.VMEM)


def greet(partners):
    barrier = pltpu.get_barrier_semaphore()
    for partner in partners:
        pl.semaphore_signal(barrier, inc=1, device_id=partner, device_id_type=MESH)
    pl.semaphore_wait(barrier, len(partners))


def push(src, dst, sems, index, partner):
    copy = pltpu.make_async_remote_copy(
        src_ref=src,
        dst_ref=dst,
        send_sem=sems[0].at[index],
        recv_sem=sems[1].at[index],
        device_id=partner,
        device_id_type=MESH,
    )
    copy.start()
    return copy


def dom_partners(doms):
    group, dom = lax.axis_index("group"), lax.axis_index("dom")
    chips = doms // 2
    chip, core = dom // 2, dom % 2
    other = chip * 2 + (1 - core)
    ahead = [lax.rem(chip + k, chips) * 2 + core for k in range(1, chips)]
    behind = [lax.rem(chip + chips - k, chips) for k in range(1, chips)]
    return group, dom, core, other, ahead, behind


def gather_kernel(
    groups, doms, unit_ref, requests_ref, table_ref, asked_ref,
    own_sem, near_send, near_recv, far_send, far_recv, on_send, on_recv, ask_send, ask_recv,
):
    group, dom, core, other, ahead, behind = dom_partners(doms)
    count = unit_ref.shape[0]
    peers = [lax.rem(group + k, groups) for k in range(1, groups)]
    greet([(group, other)] + [(group, far) for far in ahead] + [(peer, dom) for peer in peers])
    here = table_ref.at[rows_of(dom, count), :]
    far_copies = [
        push(unit_ref, here, (far_send, far_recv), k, (group, far)) for k, far in enumerate(ahead)
    ]
    ask_copies = [
        push(requests_ref.at[peer], asked_ref.at[group], (ask_send, ask_recv), k, (peer, dom))
        for k, peer in enumerate(peers)
    ]
    near = push(unit_ref, here, (near_send, near_recv), 0, (group, other))
    own = pltpu.make_async_copy(unit_ref, here, own_sem.at[0])
    own.start()
    own_ask = pltpu.make_async_copy(requests_ref.at[group], asked_ref.at[group], own_sem.at[1])
    own_ask.start()
    on_copies = []
    for k, copy in enumerate(far_copies):
        copy.wait_recv()
        block = table_ref.at[rows_of(behind[k] * 2 + core, count), :]
        on_copies.append(push(block, block, (on_send, on_recv), k, (group, other)))
    own.wait()
    own_ask.wait()
    near.wait()
    for copy in ask_copies:
        copy.wait()
    for copy in far_copies:
        copy.wait_send()
    for copy in on_copies:
        copy.wait()


def gather_table(unit_rows, own_requests, groups, doms):
    slots = own_requests.shape[1]
    asks = jnp.broadcast_to(own_requests[:, None, :], (groups, 8, slots))
    asks = jnp.pad(asks, ((0, 0), (0, 0), (0, 128 - slots)))
    far, peers = max(doms // 2 - 1, 1), max(groups - 1, 1)
    dma = pltpu.SemaphoreType.DMA
    table, asked = pl.pallas_call(
        functools.partial(gather_kernel, groups, doms),
        out_shape=(
            jax.ShapeDtypeStruct((doms * unit_rows.shape[0], unit_rows.shape[1]), unit_rows.dtype),
            jax.ShapeDtypeStruct(asks.shape, asks.dtype),
        ),
        in_specs=[ANYWHERE, ANYWHERE],
        out_specs=(ANYWHERE, ANYWHERE),
        scratch_shapes=[
            dma((2,)), dma((1,)), dma((1,)), dma((far,)), dma((far,)),
            dma((far,)), dma((far,)), dma((peers,)), dma((peers,)),
        ],
        compiler_params=pltpu.CompilerParams(collective_id=0, has_side_effects=True),
    )(unit_rows, asks)
    return table, asked[:, 0, :slots].reshape(-1)


def scatter_kernel(
    doms, merged_ref, out_ref, mine, kept, near_got, far_out, far_got,
    own_sem, near_send, near_recv, far_send, far_recv,
):
    group, dom, core, other, ahead, behind = dom_partners(doms)
    count = out_ref.shape[0]
    chips = doms // 2
    greet([(group, other)] + [(group, far) for far in ahead])
    order = [dom // 2] + [lax.rem(dom // 2 + k, chips) for k in range(1, chips)]
    order = order[1:] + order[:1]
    near_copies = []
    own_copies = []
    for k, chip in enumerate(order):
        theirs = merged_ref.at[rows_of(chip * 2 + (1 - core), count), :]
        near_copies.append(push(theirs, near_got.at[k], (near_send, near_recv), k, (group, other)))
        ours = merged_ref.at[rows_of(chip * 2 + core, count), :]
        copy = pltpu.make_async_copy(ours, mine.at[k], own_sem.at[k])
        copy.start()
        own_copies.append(copy)
    far_copies = []
    for k in range(chips - 1):
        near_copies[k].wait_recv()
        own_copies[k].wait()
        total = mine[k].astype(jnp.float32) + near_got[k].astype(jnp.float32)
        far_out[k] = total.astype(jnp.bfloat16)
        far_copies.append(
            push(far_out.at[k], far_got.at[k], (far_send, far_recv), k, (group, ahead[k]))
        )
    near_copies[chips - 1].wait_recv()
    own_copies[chips - 1].wait()
    kept[...] = mine[chips - 1].astype(jnp.float32) + near_got[chips - 1].astype(jnp.float32)
    for k, copy in enumerate(far_copies):
        copy.wait_recv()
        kept[...] += far_got[k].astype(jnp.float32)
    out_ref[...] = kept[...]
    for copy in near_copies + far_copies:
        copy.wait_send()


def scatter_sums(merged, doms):
    count, width = merged.shape[0] // doms, merged.shape[1]
    chips = doms // 2
    far = max(chips - 1, 1)
    dma = pltpu.SemaphoreType.DMA
    return pl.pallas_call(
        functools.partial(scatter_kernel, doms),
        out_shape=jax.ShapeDtypeStruct((count, width), jnp.float32),
        in_specs=[ANYWHERE],
        out_specs=IN_VMEM,
        scratch_shapes=[
            pltpu.VMEM((chips, count, width), jnp.bfloat16),
            pltpu.VMEM((count, width), jnp.float32),
            pltpu.VMEM((chips, count, width), jnp.bfloat16),
            pltpu.VMEM((far, count, width), jnp.bfloat16),
            pltpu.VMEM((far, count, width), jnp.bfloat16),
            dma((chips,)), dma((chips,)), dma((chips,)), dma((far,)), dma((far,)),
        ],
        compiler_params=pltpu.CompilerParams(
            collective_id=1, has_side_effects=True, vmem_limit_bytes=VMEM_LIMIT
        ),
    )(merged)


def totals_kernel(
    groups, doms, x_ref, out_ref, out1, got1, part, out2, got2, gather1, gather2,
    send1, recv1, send2, recv2, send3, recv3, send4, recv4,
):
    group, dom = lax.axis_index("group"), lax.axis_index("dom")
    wide = x_ref.shape[0] // doms
    thin = wide // groups
    dom_peers = [lax.rem(dom + k, doms) for k in range(1, doms)]
    group_peers = [lax.rem(group + k, groups) for k in range(1, groups)]
    greet([(group, peer) for peer in dom_peers] + [(peer, dom) for peer in group_peers])
    copies = []
    first = []
    for k, peer in enumerate(dom_peers):
        out1[k] = x_ref[rows_of(peer, wide), :].astype(jnp.bfloat16)
        first.append(push(out1.at[k], got1.at[k], (send1, recv1), k, (group, peer)))
    part[...] = x_ref[rows_of(dom, wide), :]
    for k, copy in enumerate(first):
        copy.wait_recv()
        part[...] += got1[k].astype(jnp.float32)
    copies += first
    second = []
    for k, peer in enumerate(group_peers):
        out2[k] = part[rows_of(peer, thin), :].astype(jnp.bfloat16)
        second.append(push(out2.at[k], got2.at[k], (send2, recv2), k, (peer, dom)))
    total = part[rows_of(group, thin), :]
    for k, copy in enumerate(second):
        copy.wait_recv()
        total = total + got2[k].astype(jnp.float32)
    copies += second
    gather1[group] = (total * (1.0 / (groups * doms))).astype(jnp.bfloat16)
    mine = gather1.at[group]
    third = [
        push(mine, mine, (send3, recv3), k, (peer, dom)) for k, peer in enumerate(group_peers)
    ]
    for copy in third:
        copy.wait_recv()
    copies += third
    fourth = [
        push(gather1, gather2.at[dom], (send4, recv4), k, (group, peer))
        for k, peer in enumerate(dom_peers)
    ]
    out_ref[dom] = gather1[...].astype(jnp.float32)
    for k, copy in enumerate(fourth):
        copy.wait_recv()
        source = lax.rem(dom + doms - (k + 1), doms)
        out_ref[source] = gather2[source].astype(jnp.float32)
    copies += fourth
    for copy in copies:
        copy.wait_send()


def mean_over_devices(x, groups, doms):
    rows, width = x.shape
    wide = rows // doms
    thin = wide // groups
    a, b = max(doms - 1, 1), max(groups - 1, 1)
    half = jnp.bfloat16
    dma = pltpu.SemaphoreType.DMA
    out = pl.pallas_call(
        functools.partial(totals_kernel, groups, doms),
        out_shape=jax.ShapeDtypeStruct((doms, groups, thin, width), jnp.float32),
        in_specs=[IN_VMEM],
        out_specs=IN_VMEM,
        scratch_shapes=[
            pltpu.VMEM((a, wide, width), half),
            pltpu.VMEM((a, wide, width), half),
            pltpu.VMEM((wide, width), jnp.float32),
            pltpu.VMEM((b, thin, width), half),
            pltpu.VMEM((b, thin, width), half),
            pltpu.VMEM((groups, thin, width), half),
            pltpu.VMEM((doms, groups, thin, width), half),
            dma((a,)), dma((a,)), dma((b,)), dma((b,)), dma((b,)), dma((b,)), dma((a,)), dma((a,)),
        ],
        compiler_params=pltpu.CompilerParams(
            collective_id=2, has_side_effects=True, vmem_limit_bytes=VMEM_LIMIT
        ),
    )(x)
    return out.reshape(rows, width)


def shards(
    features, w_in, b_in, w_out, anchor_ids, local_tiles, requests, counts, remote_refs, teacher
):
    groups = lax.axis_size("group")
    doms = lax.axis_size("dom")
    devices = groups * doms
    own_requests = requests[0, 0]
    own_counts = counts[0, 0]
    slot_count = own_requests.shape[1]
    pre_act, hidden, embedding, spread, unit_rows = node_forward(features, w_in, b_in, w_out)
    table, asked = gather_table(unit_rows, own_requests, groups, doms)
    served = pick_tiles(asked, table, groups * slot_count)
    fetched = lax.all_to_all(served, "group", split_axis=0, concat_axis=0, tiled=True)
    per_step = math.gcd(local_tiles.shape[0], 2)
    prepared = prepare(
        per_step, anchor_ids, remote_refs, local_tiles.shape[1], own_counts, table, teacher,
        slot_count,
    )
    anchor_kl, delta, remote_grad = score(
        per_step, local_tiles, remote_refs, own_counts, table, fetched, prepared, slot_count
    )
    anchor_kl = anchor_kl.reshape(-1)
    returned = lax.all_to_all(remote_grad, "group", split_axis=0, concat_axis=0, tiled=True)
    local_grad = local_grads(
        per_step, anchor_ids, local_tiles, remote_refs, table, fetched, prepared[0], delta
    )
    merged = merge(asked, local_grad, returned)
    node_grad = scatter_sums(merged, doms)
    normed = embedding / spread
    embed_grad = (
        (node_grad - normed * jnp.mean(node_grad * normed, axis=1, keepdims=True)) / spread
    ).astype(jnp.bfloat16)
    out_grad = jnp.dot(hidden.T, embed_grad, preferred_element_type=jnp.float32)
    hidden_grad = jnp.dot(embed_grad, w_out.T, preferred_element_type=jnp.float32)
    sigmoid_pre = jax.nn.sigmoid(pre_act)
    pre_grad = hidden_grad * sigmoid_pre * (1.0 + pre_act * (1.0 - sigmoid_pre))
    bias_grad = jnp.sum(pre_grad, axis=0)
    in_grad_t = jnp.dot(
        pre_grad.astype(jnp.bfloat16).T, features, preferred_element_type=jnp.float32
    )
    hid = in_grad_t.shape[0]
    width = out_grad.shape[1]
    bias_rows = bias_grad.reshape(-1, width)
    used = 2 * hid + bias_rows.shape[0]
    unit = devices * 16
    padding = -used % unit
    stacked = jnp.concatenate(
        [in_grad_t, out_grad, bias_rows, jnp.zeros((padding, width), jnp.float32)], axis=0
    )
    totals = mean_over_devices(stacked, groups, doms)
    return (
        anchor_kl,
        node_grad,
        totals[:hid].T,
        totals[2 * hid : used].reshape(-1),
        totals[hid : 2 * hid],
    )


def solution(mesh):
    return jax.shard_map(
        shards,
        mesh=mesh,
        in_specs=(
            P(("group", "dom"), None),
            P(),
            P(),
            P(),
            P(("group", "dom")),
            P(("group", "dom"), None),
            P("group", "dom", None, None),
            P("group", "dom", None),
            P(("group", "dom"), None),
            P(("group", "dom"), None),
        ),
        out_specs=(P(("group", "dom")), P(("group", "dom"), None), P(), P(), P()),
        check_vma=False,
    )
```

```python
import functools
import math

import jax
import jax.numpy as jnp
from jax import lax
from jax.experimental import pallas as pl
from jax.experimental.pallas import tpu as pltpu
from jax.sharding import PartitionSpec as P

TILE = 128
ABLK = 128

SCORE_SCALE = 8.0
EPSILON = 1e-06
VMEM_LIMIT = 60 * 1024 * 1024
CHUNK = 256

ONE_COPY = pl.Buffered(1)


def whole(shape):
    return pl.BlockSpec(shape, lambda *_: (0,) * len(shape), pipeline_mode=ONE_COPY)


def node_forward(feature_rows, w_in, b_in, w_out):
    pre_act = jnp.dot(feature_rows, w_in, preferred_element_type=jnp.float32) + b_in
    hidden = jax.nn.silu(pre_act).astype(jnp.bfloat16)
    embedding = jnp.dot(hidden, w_out, preferred_element_type=jnp.float32)
    spread = jnp.sqrt(jnp.mean(embedding * embedding, axis=1, keepdims=True) + EPSILON)
    unit_rows = (embedding / spread).astype(jnp.bfloat16)
    return (pre_act, hidden, embedding, spread, unit_rows)


def rows_of(index, count=TILE):
    return pl.ds(pl.multiple_of(index * count, count), count)


def pick_kernel(asked_ref, table_ref, out_ref):
    def step(slot, carry):
        out_ref[rows_of(slot), :] = table_ref[rows_of(asked_ref[slot]), :]
        return carry

    lax.fori_loop(0, out_ref.shape[0] // TILE, step, 0, unroll=2)


def pick_tiles(asked, table, slots):
    shape = (slots * TILE, table.shape[1])
    return pl.pallas_call(
        pick_kernel,
        out_shape=jax.ShapeDtypeStruct(shape, table.dtype),
        grid_spec=pltpu.PrefetchScalarGridSpec(
            num_scalar_prefetch=1,
            grid=(1,),
            in_specs=[whole(table.shape)],
            out_specs=whole(shape),
        ),
        compiler_params=pltpu.CompilerParams(vmem_limit_bytes=VMEM_LIMIT),
    )(asked, table)


def cost(flops, moved, powers):
    return pl.CostEstimate(flops=flops, bytes_accessed=moved, transcendentals=powers)


def clear_rows(ref):
    zero_chunk = jnp.zeros((CHUNK, ref.shape[1]), ref.dtype)

    def clear(index, carry):
        ref[rows_of(index, CHUNK), :] = zero_chunk
        return carry

    lax.fori_loop(0, ref.shape[0] // CHUNK, clear, 0)


def as_row(column):
    return jnp.broadcast_to(column, (ABLK, TILE)).T[0:1, :]


def as_column(row):
    return jnp.broadcast_to(row, (TILE, ABLK)).T[:, 0:1]


def tile_scores(anchors, context):
    return lax.dot_general(
        anchors, context, (((1,), (1,)), ((), ())), preferred_element_type=jnp.float32
    )


def prepare_kernel(
    per_step, local_count, remote_count, slot_count, ids_ref, tiles_ref, refs_ref, counts_ref,
    table_ref, teacher_ref, anchors_ref, near_ref, far_ref, base_ref, partial_ref,
    table_f, anchor_rows,
):
    scale = SCORE_SCALE / table_ref.shape[1]

    @pl.when(pl.program_id(0) == 0)
    def _():
        def widen(index, carry):
            here = rows_of(index, CHUNK)
            table_f[here, :] = table_ref[here, :].astype(jnp.float32)
            return carry

        lax.fori_loop(0, table_f.shape[0] // CHUNK, widen, 0)

    for sub in range(per_step):
        block = pl.program_id(0) * per_step + sub
        rows = slice(sub * ABLK, (sub + 1) * ABLK)
        for row in range(ABLK):
            at = sub * ABLK + row
            index = ids_ref[block * ABLK + row]
            anchor_rows[at : at + 1, :] = table_f[pl.ds(index, 1), :]
        anchors = (anchor_rows[rows, :] * scale).astype(jnp.bfloat16)
        anchors_ref[rows, :] = anchors
        target_sum = gap_sum = student_sum = None
        exps = []
        for i in range(local_count + remote_count):
            teacher = teacher_ref[rows, i * TILE : (i + 1) * TILE].astype(jnp.float32)
            target_exp = jnp.exp(teacher)
            if i >= local_count:
                ref = refs_ref[block * remote_count + i - local_count]
                live = lax.rem(ref, slot_count) < counts_ref[lax.div(ref, slot_count)]
                target_exp = target_exp * jnp.where(live, 1.0, 0.0).astype(jnp.float32)
                gap = target_exp * teacher
            else:
                place = rows_of(tiles_ref[block * local_count + i])
                scores = tile_scores(anchors, table_ref[place, :])
                gap = target_exp * (teacher - scores)
                student_exp = jnp.exp(scores)
                student_sum = student_exp if i == 0 else student_sum + student_exp
            target_sum = target_exp if i == 0 else target_sum + target_exp
            gap_sum = gap if i == 0 else gap_sum + gap
            exps.append(target_exp)
        total = jnp.sum(target_sum, axis=1, keepdims=True)
        inverse = 1.0 / total
        base = jnp.sum(gap_sum, axis=1, keepdims=True) * inverse - jnp.log(total)
        base_ref[sub] = as_row(base)
        partial_ref[sub] = as_row(jnp.sum(student_sum, axis=1, keepdims=True))
        for i, target_exp in enumerate(exps):
            out_ref, at = (near_ref, i) if i < local_count else (far_ref, i - local_count)
            out_ref[rows, at * TILE : (at + 1) * TILE] = (target_exp * inverse).astype(
                jnp.bfloat16
            )


def prepare(per_step, anchor_ids, local_tiles, remote_refs, own_counts, table, teacher, slots):
    blocks, remote_count = remote_refs.shape
    local_count = local_tiles.shape[1]
    near, far = local_count * TILE, remote_count * TILE
    anchors, context_width = teacher.shape
    width = table.shape[1]
    rows = per_step * ABLK
    return pl.pallas_call(
        functools.partial(prepare_kernel, per_step, local_count, remote_count, slots),
        out_shape=(
            jax.ShapeDtypeStruct((anchors, width), jnp.bfloat16),
            jax.ShapeDtypeStruct((anchors, near), jnp.bfloat16),
            jax.ShapeDtypeStruct((anchors, far), jnp.bfloat16),
            jax.ShapeDtypeStruct((blocks, 1, ABLK), jnp.float32),
            jax.ShapeDtypeStruct((blocks, 1, ABLK), jnp.float32),
        ),
        grid_spec=pltpu.PrefetchScalarGridSpec(
            num_scalar_prefetch=4,
            grid=(blocks // per_step,),
            in_specs=[
                whole(table.shape),
                pl.BlockSpec((rows, context_width), lambda b, *_: (b, 0)),
            ],
            out_specs=(
                pl.BlockSpec((rows, width), lambda b, *_: (b, 0)),
                pl.BlockSpec((rows, near), lambda b, *_: (b, 0)),
                pl.BlockSpec((rows, far), lambda b, *_: (b, 0)),
                pl.BlockSpec((per_step, 1, ABLK), lambda b, *_: (b, 0, 0)),
                pl.BlockSpec((per_step, 1, ABLK), lambda b, *_: (b, 0, 0)),
            ),
            scratch_shapes=[
                pltpu.VMEM(table.shape, jnp.float32),
                pltpu.VMEM((rows, width), jnp.float32),
            ],
        ),
        compiler_params=pltpu.CompilerParams(vmem_limit_bytes=VMEM_LIMIT),
        cost_estimate=cost(
            10 * anchors * context_width, 4 * anchors * context_width, anchors * context_width
        ),
    )(
        anchor_ids, local_tiles.reshape(-1), remote_refs.reshape(-1), own_counts, table, teacher
    )


def take_context(block, sub, context, tiles_ref, refs_ref, table_ref, fetched_ref, counts):
    local_count, remote_count = counts
    places = []
    for i in range(local_count):
        place = rows_of(tiles_ref[block * local_count + i])
        context[sub, i * TILE : (i + 1) * TILE, :] = table_ref[place, :]
        places.append(place)
    for i in range(remote_count):
        place = rows_of(refs_ref[block * remote_count + i])
        at = local_count + i
        context[sub, at * TILE : (at + 1) * TILE, :] = fetched_ref[place, :]
        places.append(place)
    return places


def tile_grad(delta, anchors):
    return lax.dot_general(
        delta, anchors, (((0,), (0,)), ((), ())), preferred_element_type=jnp.float32
    )


def score_kernel(
    per_step, remote_count, slot_count, refs_ref, counts_ref,
    fetched_ref, anchors_ref, far_ref, base_ref, partial_ref,
    kl_ref, inverse_ref, delta_ref, remote_grad_ref, remote_acc,
):
    @pl.when(pl.program_id(0) == 0)
    def _():
        clear_rows(remote_acc)

    for sub in range(per_step):
        block = pl.program_id(0) * per_step + sub
        rows = slice(sub * ABLK, (sub + 1) * ABLK)
        anchors = anchors_ref[rows, :]
        places = []
        student = []
        student_sum = gap_sum = None
        for i in range(remote_count):
            span = slice(i * TILE, (i + 1) * TILE)
            ref = refs_ref[block * remote_count + i]
            places.append(rows_of(ref))
            live = lax.rem(ref, slot_count) < counts_ref[lax.div(ref, slot_count)]
            scores = tile_scores(anchors, fetched_ref[places[i], :])
            student_exp = jnp.exp(scores) * jnp.where(live, 1.0, 0.0).astype(jnp.float32)
            gap = far_ref[rows, span].astype(jnp.float32) * scores
            student_sum = student_exp if i == 0 else student_sum + student_exp
            gap_sum = gap if i == 0 else gap_sum + gap
            student.append(student_exp)
        total = as_column(partial_ref[sub]) + jnp.sum(student_sum, axis=1, keepdims=True)
        inverse = 1.0 / total
        rest = jnp.log(total) - jnp.sum(gap_sum, axis=1, keepdims=True)
        kl_ref[sub] = base_ref[sub] + as_row(rest)
        inverse_ref[sub] = as_row(inverse)
        for i in range(remote_count):
            span = slice(i * TILE, (i + 1) * TILE)
            delta = (student[i] * inverse - far_ref[rows, span].astype(jnp.float32)).astype(
                jnp.bfloat16
            )
            delta_ref[rows, span] = delta
            remote_acc[places[i], :] += tile_grad(delta, anchors)

    @pl.when(pl.program_id(0) == pl.num_programs(0) - 1)
    def _():
        def finish(index, carry):
            here = rows_of(index, CHUNK)
            remote_grad_ref[here, :] = remote_acc[here, :].astype(jnp.bfloat16)
            return carry

        lax.fori_loop(0, remote_acc.shape[0] // CHUNK, finish, 0)


def score(per_step, remote_refs, own_counts, fetched, prepared, slots):
    anchors, near, far, base, partial = prepared
    blocks, remote_count = remote_refs.shape
    width = anchors.shape[1]
    rows = per_step * ABLK
    pairs = far.shape[0] * far.shape[1]
    row_spec = pl.BlockSpec((per_step, 1, ABLK), lambda b, *_: (b, 0, 0))
    far_spec = pl.BlockSpec((rows, far.shape[1]), lambda b, *_: (b, 0))
    return pl.pallas_call(
        functools.partial(score_kernel, per_step, remote_count, slots),
        out_shape=(
            jax.ShapeDtypeStruct((blocks, 1, ABLK), jnp.float32),
            jax.ShapeDtypeStruct((blocks, 1, ABLK), jnp.float32),
            jax.ShapeDtypeStruct(far.shape, jnp.bfloat16),
            jax.ShapeDtypeStruct(fetched.shape, jnp.bfloat16),
        ),
        grid_spec=pltpu.PrefetchScalarGridSpec(
            num_scalar_prefetch=2,
            grid=(blocks // per_step,),
            in_specs=[
                whole(fetched.shape),
                pl.BlockSpec((rows, width), lambda b, *_: (b, 0)),
                far_spec,
                row_spec,
                row_spec,
            ],
            out_specs=(row_spec, row_spec, far_spec, whole(fetched.shape)),
            scratch_shapes=[pltpu.VMEM(fetched.shape, jnp.float32)],
        ),
        compiler_params=pltpu.CompilerParams(vmem_limit_bytes=VMEM_LIMIT),
        cost_estimate=cost(3 * pairs * width, 4 * pairs, pairs),
    )(remote_refs.reshape(-1), own_counts, fetched, anchors, far, base, partial)


def local_kernel(
    per_step, local_count, remote_count, lanes, ids_ref, tiles_ref, refs_ref,
    table_ref, fetched_ref, anchors_ref, near_ref, inverse_ref, delta_ref, local_grad_ref,
    context, near_delta, anchor_grad, *row_accs,
):
    scale = SCORE_SCALE / table_ref.shape[1]

    @pl.when(pl.program_id(0) == 0)
    def _():
        clear_rows(local_grad_ref)
        for acc in row_accs:
            clear_rows(acc)

    for sub in range(per_step):
        block = pl.program_id(0) * per_step + sub
        rows = slice(sub * ABLK, (sub + 1) * ABLK)
        places = take_context(
            block, sub, context, tiles_ref, refs_ref, table_ref, fetched_ref,
            (local_count, remote_count),
        )
        anchors = anchors_ref[rows, :]
        inverse = as_column(inverse_ref[sub])
        near = local_count * TILE
        for i in range(local_count):
            span = slice(i * TILE, (i + 1) * TILE)
            student = jnp.exp(tile_scores(anchors, context[sub, span, :])) * inverse
            delta = (student - near_ref[rows, span].astype(jnp.float32)).astype(jnp.bfloat16)
            near_delta[rows, span] = delta
            local_grad_ref[places[i], :] += tile_grad(delta, anchors)
        near_part = jnp.dot(
            near_delta[rows, :], context[sub, :near, :], preferred_element_type=jnp.float32
        )
        far_part = jnp.dot(
            delta_ref[rows, :], context[sub, near:, :], preferred_element_type=jnp.float32
        )
        anchor_grad[rows, :] = (near_part + far_part) * scale
        for row in range(ABLK):
            acc = row_accs[row % lanes]
            at = sub * ABLK + row
            acc[pl.ds(ids_ref[block * ABLK + row], 1), :] += anchor_grad[at : at + 1, :]

    @pl.when(pl.program_id(0) == pl.num_programs(0) - 1)
    def _():
        def finish(index, carry):
            here = rows_of(index, CHUNK)
            total = local_grad_ref[here, :]
            for acc in row_accs:
                total = total + acc[here, :]
            local_grad_ref[here, :] = total
            return carry

        lax.fori_loop(0, local_grad_ref.shape[0] // CHUNK, finish, 0)


def local_grads(
    per_step, anchor_ids, local_tiles, remote_refs, table, fetched, anchors, near, inverse, delta
):
    blocks, local_count = local_tiles.shape
    remote_count = remote_refs.shape[1]
    context_width = near.shape[1] + delta.shape[1]
    width = table.shape[1]
    rows = per_step * ABLK
    lanes = 4 if table.shape[0] <= 8192 else 1
    pairs = delta.shape[0] * context_width
    return pl.pallas_call(
        functools.partial(local_kernel, per_step, local_count, remote_count, lanes),
        out_shape=jax.ShapeDtypeStruct(table.shape, jnp.float32),
        grid_spec=pltpu.PrefetchScalarGridSpec(
            num_scalar_prefetch=3,
            grid=(blocks // per_step,),
            in_specs=[
                whole(table.shape),
                whole(fetched.shape),
                pl.BlockSpec((rows, width), lambda b, *_: (b, 0)),
                pl.BlockSpec((rows, near.shape[1]), lambda b, *_: (b, 0)),
                pl.BlockSpec((per_step, 1, ABLK), lambda b, *_: (b, 0, 0)),
                pl.BlockSpec((rows, delta.shape[1]), lambda b, *_: (b, 0)),
            ],
            out_specs=whole(table.shape),
            scratch_shapes=[
                pltpu.VMEM((per_step, context_width, width), jnp.bfloat16),
                pltpu.VMEM((rows, near.shape[1]), jnp.bfloat16),
                pltpu.VMEM((rows, width), jnp.float32),
            ]
            + [pltpu.VMEM(table.shape, jnp.float32)] * lanes,
        ),
        compiler_params=pltpu.CompilerParams(vmem_limit_bytes=VMEM_LIMIT),
        cost_estimate=cost(3 * pairs * width, 2 * pairs, 0),
    )(
        anchor_ids, local_tiles.reshape(-1), remote_refs.reshape(-1),
        table, fetched, anchors, near, inverse, delta,
    )


def merge_kernel(asked_ref, local_ref, returned_ref, out_ref, acc):
    def load(index, carry):
        here = rows_of(index, CHUNK)
        acc[here, :] = local_ref[here, :]
        return carry

    lax.fori_loop(0, acc.shape[0] // CHUNK, load, 0)

    def add(slot, carry):
        acc[rows_of(asked_ref[slot]), :] += returned_ref[rows_of(slot), :].astype(jnp.float32)
        return carry

    lax.fori_loop(0, returned_ref.shape[0] // TILE, add, 0)

    def store(index, carry):
        here = rows_of(index, CHUNK)
        out_ref[here, :] = acc[here, :].astype(jnp.bfloat16)
        return carry

    lax.fori_loop(0, acc.shape[0] // CHUNK, store, 0)


def merge(asked, local_grad, returned):
    return pl.pallas_call(
        merge_kernel,
        out_shape=jax.ShapeDtypeStruct(local_grad.shape, jnp.bfloat16),
        grid_spec=pltpu.PrefetchScalarGridSpec(
            num_scalar_prefetch=1,
            grid=(1,),
            in_specs=[whole(local_grad.shape), whole(returned.shape)],
            out_specs=whole(local_grad.shape),
            scratch_shapes=[pltpu.VMEM(local_grad.shape, jnp.float32)],
        ),
        compiler_params=pltpu.CompilerParams(vmem_limit_bytes=VMEM_LIMIT),
    )(asked, local_grad, returned)


MESH = pl.DeviceIdType.MESH
ANYWHERE = pl.BlockSpec(memory_space=pl.ANY)
IN_VMEM = pl.BlockSpec(memory_space=pltpu.VMEM)


def greet(partners):
    barrier = pltpu.get_barrier_semaphore()
    for partner in partners:
        pl.semaphore_signal(barrier, inc=1, device_id=partner, device_id_type=MESH)
    pl.semaphore_wait(barrier, len(partners))


def push(src, dst, sems, index, partner):
    copy = pltpu.make_async_remote_copy(
        src_ref=src,
        dst_ref=dst,
        send_sem=sems[0].at[index],
        recv_sem=sems[1].at[index],
        device_id=partner,
        device_id_type=MESH,
    )
    copy.start()
    return copy


def dom_partners(doms):
    group, dom = lax.axis_index("group"), lax.axis_index("dom")
    chips = doms // 2
    chip, core = dom // 2, dom % 2
    other = chip * 2 + (1 - core)
    ahead = [lax.rem(chip + k, chips) * 2 + core for k in range(1, chips)]
    behind = [lax.rem(chip + chips - k, chips) for k in range(1, chips)]
    return group, dom, core, other, ahead, behind


def gather_kernel(
    groups, doms, unit_ref, requests_ref, table_ref, asked_ref,
    own_sem, near_send, near_recv, far_send, far_recv, on_send, on_recv, ask_send, ask_recv,
):
    group, dom, core, other, ahead, behind = dom_partners(doms)
    count = unit_ref.shape[0]
    peers = [lax.rem(group + k, groups) for k in range(1, groups)]
    greet([(group, other)] + [(group, far) for far in ahead] + [(peer, dom) for peer in peers])
    here = table_ref.at[rows_of(dom, count), :]
    far_copies = [
        push(unit_ref, here, (far_send, far_recv), k, (group, far)) for k, far in enumerate(ahead)
    ]
    ask_copies = [
        push(requests_ref.at[peer], asked_ref.at[group], (ask_send, ask_recv), k, (peer, dom))
        for k, peer in enumerate(peers)
    ]
    near = push(unit_ref, here, (near_send, near_recv), 0, (group, other))
    own = pltpu.make_async_copy(unit_ref, here, own_sem.at[0])
    own.start()
    own_ask = pltpu.make_async_copy(requests_ref.at[group], asked_ref.at[group], own_sem.at[1])
    own_ask.start()
    on_copies = []
    for k, copy in enumerate(far_copies):
        copy.wait_recv()
        block = table_ref.at[rows_of(behind[k] * 2 + core, count), :]
        on_copies.append(push(block, block, (on_send, on_recv), k, (group, other)))
    own.wait()
    own_ask.wait()
    near.wait()
    for copy in ask_copies:
        copy.wait()
    for copy in far_copies:
        copy.wait_send()
    for copy in on_copies:
        copy.wait()


def gather_table(unit_rows, own_requests, groups, doms):
    slots = own_requests.shape[1]
    asks = jnp.broadcast_to(own_requests[:, None, :], (groups, 8, slots))
    asks = jnp.pad(asks, ((0, 0), (0, 0), (0, 128 - slots)))
    far, peers = max(doms // 2 - 1, 1), max(groups - 1, 1)
    dma = pltpu.SemaphoreType.DMA
    table, asked = pl.pallas_call(
        functools.partial(gather_kernel, groups, doms),
        out_shape=(
            jax.ShapeDtypeStruct((doms * unit_rows.shape[0], unit_rows.shape[1]), unit_rows.dtype),
            jax.ShapeDtypeStruct(asks.shape, asks.dtype),
        ),
        in_specs=[ANYWHERE, ANYWHERE],
        out_specs=(ANYWHERE, ANYWHERE),
        scratch_shapes=[
            dma((2,)), dma((1,)), dma((1,)), dma((far,)), dma((far,)),
            dma((far,)), dma((far,)), dma((peers,)), dma((peers,)),
        ],
        compiler_params=pltpu.CompilerParams(collective_id=0, has_side_effects=True),
    )(unit_rows, asks)
    return table, asked[:, 0, :slots].reshape(-1)


def scatter_kernel(
    doms, merged_ref, out_ref, mine, kept, near_got, far_out, far_got,
    own_sem, near_send, near_recv, far_send, far_recv,
):
    group, dom, core, other, ahead, behind = dom_partners(doms)
    count = out_ref.shape[0]
    chips = doms // 2
    greet([(group, other)] + [(group, far) for far in ahead])
    order = [dom // 2] + [lax.rem(dom // 2 + k, chips) for k in range(1, chips)]
    order = order[1:] + order[:1]
    near_copies = []
    own_copies = []
    for k, chip in enumerate(order):
        theirs = merged_ref.at[rows_of(chip * 2 + (1 - core), count), :]
        near_copies.append(push(theirs, near_got.at[k], (near_send, near_recv), k, (group, other)))
        ours = merged_ref.at[rows_of(chip * 2 + core, count), :]
        copy = pltpu.make_async_copy(ours, mine.at[k], own_sem.at[k])
        copy.start()
        own_copies.append(copy)
    far_copies = []
    for k in range(chips - 1):
        near_copies[k].wait_recv()
        own_copies[k].wait()
        total = mine[k].astype(jnp.float32) + near_got[k].astype(jnp.float32)
        far_out[k] = total.astype(jnp.bfloat16)
        far_copies.append(
            push(far_out.at[k], far_got.at[k], (far_send, far_recv), k, (group, ahead[k]))
        )
    near_copies[chips - 1].wait_recv()
    own_copies[chips - 1].wait()
    kept[...] = mine[chips - 1].astype(jnp.float32) + near_got[chips - 1].astype(jnp.float32)
    for k, copy in enumerate(far_copies):
        copy.wait_recv()
        kept[...] += far_got[k].astype(jnp.float32)
    out_ref[...] = kept[...]
    for copy in near_copies + far_copies:
        copy.wait_send()


def scatter_sums(merged, doms):
    count, width = merged.shape[0] // doms, merged.shape[1]
    chips = doms // 2
    far = max(chips - 1, 1)
    dma = pltpu.SemaphoreType.DMA
    return pl.pallas_call(
        functools.partial(scatter_kernel, doms),
        out_shape=jax.ShapeDtypeStruct((count, width), jnp.float32),
        in_specs=[ANYWHERE],
        out_specs=IN_VMEM,
        scratch_shapes=[
            pltpu.VMEM((chips, count, width), jnp.bfloat16),
            pltpu.VMEM((count, width), jnp.float32),
            pltpu.VMEM((chips, count, width), jnp.bfloat16),
            pltpu.VMEM((far, count, width), jnp.bfloat16),
            pltpu.VMEM((far, count, width), jnp.bfloat16),
            dma((chips,)), dma((chips,)), dma((chips,)), dma((far,)), dma((far,)),
        ],
        compiler_params=pltpu.CompilerParams(
            collective_id=1, has_side_effects=True, vmem_limit_bytes=VMEM_LIMIT
        ),
    )(merged)


def totals_kernel(
    groups, doms, x_ref, out_ref, out1, got1, part, out2, got2, gather1, gather2,
    send1, recv1, send2, recv2, send3, recv3, send4, recv4,
):
    group, dom = lax.axis_index("group"), lax.axis_index("dom")
    wide = x_ref.shape[0] // doms
    thin = wide // groups
    dom_peers = [lax.rem(dom + k, doms) for k in range(1, doms)]
    group_peers = [lax.rem(group + k, groups) for k in range(1, groups)]
    greet([(group, peer) for peer in dom_peers] + [(peer, dom) for peer in group_peers])
    copies = []
    first = []
    for k, peer in enumerate(dom_peers):
        out1[k] = x_ref[rows_of(peer, wide), :].astype(jnp.bfloat16)
        first.append(push(out1.at[k], got1.at[k], (send1, recv1), k, (group, peer)))
    part[...] = x_ref[rows_of(dom, wide), :]
    for k, copy in enumerate(first):
        copy.wait_recv()
        part[...] += got1[k].astype(jnp.float32)
    copies += first
    second = []
    for k, peer in enumerate(group_peers):
        out2[k] = part[rows_of(peer, thin), :].astype(jnp.bfloat16)
        second.append(push(out2.at[k], got2.at[k], (send2, recv2), k, (peer, dom)))
    total = part[rows_of(group, thin), :]
    for k, copy in enumerate(second):
        copy.wait_recv()
        total = total + got2[k].astype(jnp.float32)
    copies += second
    gather1[group] = (total * (1.0 / (groups * doms))).astype(jnp.bfloat16)
    mine = gather1.at[group]
    third = [
        push(mine, mine, (send3, recv3), k, (peer, dom)) for k, peer in enumerate(group_peers)
    ]
    for copy in third:
        copy.wait_recv()
    copies += third
    fourth = [
        push(gather1, gather2.at[dom], (send4, recv4), k, (group, peer))
        for k, peer in enumerate(dom_peers)
    ]
    out_ref[dom] = gather1[...].astype(jnp.float32)
    for k, copy in enumerate(fourth):
        copy.wait_recv()
        source = lax.rem(dom + doms - (k + 1), doms)
        out_ref[source] = gather2[source].astype(jnp.float32)
    copies += fourth
    for copy in copies:
        copy.wait_send()


def mean_over_devices(x, groups, doms):
    rows, width = x.shape
    wide = rows // doms
    thin = wide // groups
    a, b = max(doms - 1, 1), max(groups - 1, 1)
    half = jnp.bfloat16
    dma = pltpu.SemaphoreType.DMA
    out = pl.pallas_call(
        functools.partial(totals_kernel, groups, doms),
        out_shape=jax.ShapeDtypeStruct((doms, groups, thin, width), jnp.float32),
        in_specs=[IN_VMEM],
        out_specs=IN_VMEM,
        scratch_shapes=[
            pltpu.VMEM((a, wide, width), half),
            pltpu.VMEM((a, wide, width), half),
            pltpu.VMEM((wide, width), jnp.float32),
            pltpu.VMEM((b, thin, width), half),
            pltpu.VMEM((b, thin, width), half),
            pltpu.VMEM((groups, thin, width), half),
            pltpu.VMEM((doms, groups, thin, width), half),
            dma((a,)), dma((a,)), dma((b,)), dma((b,)), dma((b,)), dma((b,)), dma((a,)), dma((a,)),
        ],
        compiler_params=pltpu.CompilerParams(
            collective_id=2, has_side_effects=True, vmem_limit_bytes=VMEM_LIMIT
        ),
    )(x)
    return out.reshape(rows, width)


def shards(
    features, w_in, b_in, w_out, anchor_ids, local_tiles, requests, counts, remote_refs, teacher
):
    groups = lax.axis_size("group")
    doms = lax.axis_size("dom")
    devices = groups * doms
    own_requests = requests[0, 0]
    own_counts = counts[0, 0]
    slot_count = own_requests.shape[1]
    pre_act, hidden, embedding, spread, unit_rows = node_forward(features, w_in, b_in, w_out)
    table, asked = gather_table(unit_rows, own_requests, groups, doms)
    served = pick_tiles(asked, table, groups * slot_count)
    fetched = lax.all_to_all(served, "group", split_axis=0, concat_axis=0, tiled=True)
    per_step = math.gcd(local_tiles.shape[0], 2)
    prepared = prepare(
        per_step, anchor_ids, local_tiles, remote_refs, own_counts, table, teacher, slot_count
    )
    anchor_kl, inverse, delta, remote_grad = score(
        per_step, remote_refs, own_counts, fetched, prepared, slot_count
    )
    anchor_kl = anchor_kl.reshape(-1)
    returned = lax.all_to_all(remote_grad, "group", split_axis=0, concat_axis=0, tiled=True)
    local_grad = local_grads(
        per_step, anchor_ids, local_tiles, remote_refs, table, fetched, prepared[0], prepared[1],
        inverse, delta,
    )
    merged = merge(asked, local_grad, returned)
    node_grad = scatter_sums(merged, doms)
    normed = embedding / spread
    embed_grad = (
        (node_grad - normed * jnp.mean(node_grad * normed, axis=1, keepdims=True)) / spread
    ).astype(jnp.bfloat16)
    out_grad = jnp.dot(hidden.T, embed_grad, preferred_element_type=jnp.float32)
    hidden_grad = jnp.dot(embed_grad, w_out.T, preferred_element_type=jnp.float32)
    sigmoid_pre = jax.nn.sigmoid(pre_act)
    pre_grad = hidden_grad * sigmoid_pre * (1.0 + pre_act * (1.0 - sigmoid_pre))
    bias_grad = jnp.sum(pre_grad, axis=0)
    in_grad_t = jnp.dot(
        pre_grad.astype(jnp.bfloat16).T, features, preferred_element_type=jnp.float32
    )
    hid = in_grad_t.shape[0]
    width = out_grad.shape[1]
    bias_rows = bias_grad.reshape(-1, width)
    used = 2 * hid + bias_rows.shape[0]
    unit = devices * 16
    padding = -used % unit
    stacked = jnp.concatenate(
        [in_grad_t, out_grad, bias_rows, jnp.zeros((padding, width), jnp.float32)], axis=0
    )
    totals = mean_over_devices(stacked, groups, doms)
    return (
        anchor_kl,
        node_grad,
        totals[:hid].T,
        totals[2 * hid : used].reshape(-1),
        totals[hid : 2 * hid],
    )


def solution(mesh):
    return jax.shard_map(
        shards,
        mesh=mesh,
        in_specs=(
            P(("group", "dom"), None),
            P(),
            P(),
            P(),
            P(("group", "dom")),
            P(("group", "dom"), None),
            P("group", "dom", None, None),
            P("group", "dom", None),
            P(("group", "dom"), None),
            P(("group", "dom"), None),
        ),
        out_specs=(P(("group", "dom")), P(("group", "dom"), None), P(), P(), P()),
        check_vma=False,
    )
```
